128 devices in a mesh: blk: 8 (over z_lo, y), tile: 16 (over x, z_hi, core).
Axes of the slice: x: 4, y: 4, z: 4 (z_hi: 2, z_lo: 2; z = z_hi * 2 + z_lo), core: 2. Of those that a mesh axis runs over, the one named last changes fastest.
Arguments:
- left_rows: bfloat16 [2048, 49152], P('blk', 'tile'), may hold values from -0.125 to 0.125
- right_rows: bfloat16 [2048, 4096], P('blk', 'tile'), may hold values from -6 to 6
- row_weight: float32 [2048], P('blk'), may hold values from 0.25 to 4
- coupling: float32 [2048], P('blk'), may hold values from -6 to 6
- assign: int32 [16], replicated, may hold values from 0 to 7, as said below
- orders: int32 [16], replicated, may hold values from 42 to 214, as said below
- offsets: int32 [16], replicated, may hold values from 0 to 214, as said below
Outputs:
- schur_band: bfloat16 [4096, 49152], P('blk', 'tile')
The draws below stay inside these ranges and needn't reach their ends.
Inputs may be any that keep to these rules, and one draw needn't show every extreme that they name: `assign`: each blk index names exactly 2 blocks. The orders of the blocks that one blk index names sum to at most 256, and to exactly 256 for some index in every draw. offsets[b] is the sum of the orders of the blocks before b in the list that name the same blk index.
All inputs are finite; a program needn't handle non-finite values.
Results may differ from the reference program's by a relative error of at most 0.013.
Values may be sent and summed in bfloat16 or wider, within the bound.
A program may use at most 128 MiB of HBM per device.

```python
import math
import jax
import jax.numpy as jnp
from jax import lax

DUAL = 49152
BAND = 4096
CAP = 256
BLK_DEV = 2
NBLOCKS = 16
ROWS = 2048
N_BLK = 8


def layout_draw(base_key):
    least_rows = CAP // 6
    key_first = jax.random.fold_in(base_key, 11)
    key_second = jax.random.fold_in(base_key, 12)
    key_third = jax.random.fold_in(base_key, 13)
    shuffled = jax.random.permutation(key_first, NBLOCKS)
    assign = (shuffled // BLK_DEV).astype(jnp.int32)
    block_ids = jnp.arange(NBLOCKS, dtype=jnp.int32)
    same_dev = assign[None, :] == assign[:, None]
    earlier = block_ids[None, :] < block_ids[:, None]
    before_count = jnp.sum((same_dev & earlier).astype(jnp.int32), axis=1)
    is_first = before_count == 0
    first_draw = jax.random.randint(key_second, (NBLOCKS,), least_rows, CAP - least_rows + 1, dtype=jnp.int32)
    first_draw = jnp.where(block_ids == 0, CAP - least_rows, first_draw).astype(jnp.int32)
    first_orders = jnp.where(is_first, first_draw, 0).astype(jnp.int32)
    partner_first = jnp.sum(jnp.where(same_dev & earlier, first_orders[None, :], 0), axis=1).astype(jnp.int32)
    raw_second = jax.random.randint(key_third, (NBLOCKS,), 0, 1048576, dtype=jnp.int32)
    second_span = CAP - partner_first - least_rows + 1
    second_orders = least_rows + raw_second % jnp.maximum(second_span, 1)
    orders = jnp.where(is_first, first_draw, second_orders).astype(jnp.int32)
    offsets = jnp.sum(jnp.where(same_dev & earlier, orders[None, :], 0), axis=1).astype(jnp.int32)
    return (assign, orders, offsets)


def draw_assign(key, part):
    return layout_draw(key)[0]


def draw_orders(key, part):
    return layout_draw(key)[1]


def draw_offsets(key, part):
    return layout_draw(key)[2]


def block_scale(own_key, shape, cuts, least, top_value):
    loudness, own = 1.0, jax.random.fold_in(own_key, 6)
    for dim, shards_of in cuts:
        steps = jnp.exp(jax.random.uniform(jax.random.fold_in(own, dim), (shards_of,), jnp.float32, least / len(cuts), top_value / len(cuts)))
        loudness = loudness * jnp.repeat(steps, shape[dim] // shards_of).reshape([-1 if axis == dim else 1 for axis in range(len(shape))])
    return loudness


def centred(key, dims, scale, most, shards=(), kind=jnp.bfloat16):
    result = scale * jax.random.normal(key, dims, jnp.float32)
    if shards:
        result = result * block_scale(key, dims, shards, -0.22, 0.18)
    return jnp.clip(result, -most, most).astype(kind)


def setup_inputs(seed: int = 0) -> dict:
    keys = jax.random.split(jax.random.key(seed), 8)
    left_rows = centred(keys[0], (ROWS, DUAL), (CAP * N_BLK) ** -0.5, 0.125, ((0, 8), (1, 16)))
    right_rows = centred(keys[1], (ROWS, BAND), 1.0, 6.0, ((0, 8), (1, 16)))
    row_weight = jnp.clip(jnp.exp(math.log(4.0) - 2.7725887 * jax.random.uniform(keys[2], (ROWS,), jnp.float32) ** block_scale(keys[2], (ROWS,), ((0, 8),), -0.2, 0.2)), 0.25, 4.0)
    coupling = centred(keys[3], (ROWS,), 1.0, 6.0, ((0, 8),), jnp.float32)
    assign = draw_assign(jax.random.fold_in(keys[7], 71), 0)
    orders = draw_orders(jax.random.fold_in(keys[7], 71), 0)
    offsets = draw_offsets(jax.random.fold_in(keys[7], 71), 0)
    return {"left_rows": left_rows, "right_rows": right_rows, "row_weight": row_weight, "coupling": coupling, "assign": assign, "orders": orders, "offsets": offsets}


def reference(left_rows, right_rows, row_weight, coupling, assign, orders, offsets):
    total_rows = left_rows.shape[0]
    height = total_rows // N_BLK
    row_index = jnp.arange(total_rows, dtype=jnp.int32)
    owner_dev = row_index // height
    local_row = row_index % height
    member = ((owner_dev[:, None] == assign[None, :]) & (local_row[:, None] >= offsets[None, :]) & (local_row[:, None] < offsets[None, :] + orders[None, :])).astype(jnp.float32)
    is_live = lax.optimization_barrier(jnp.sum(member, axis=1, keepdims=True))
    right_wide = right_rows.astype(jnp.float32)
    block_sums = jnp.dot(member.T, coupling[:, None] * right_wide, precision=lax.Precision.HIGHEST)
    block_terms = block_sums / jnp.sqrt(orders.astype(jnp.float32))[:, None]
    spread_back = jnp.dot(member, block_terms, precision=lax.Precision.HIGHEST)
    weighted = (is_live * row_weight[:, None] * right_wide + coupling[:, None] * spread_back).astype(jnp.bfloat16)
    left_slabs = left_rows.reshape(N_BLK, height, left_rows.shape[1])
    weighted_slabs = weighted.reshape(N_BLK, height, weighted.shape[1])

    def add_slab(running, slab_pair):
        slab_term = lax.dot_general(slab_pair[1], slab_pair[0], (((0,), (0,)), ((), ())), preferred_element_type=jnp.float32)
        slab_term = lax.optimization_barrier(slab_term.astype(jnp.bfloat16)).astype(jnp.float32)
        return (running + slab_term, None)
    running, _ = lax.scan(add_slab, jnp.zeros((BAND, DUAL), jnp.float32), (left_slabs, weighted_slabs))
    return running.astype(jnp.bfloat16)
```

```python
import functools

import jax
import jax.numpy as jnp
from jax import lax
from jax.experimental import pallas as pl
from jax.experimental.pallas import tpu as pltpu
from jax.sharding import PartitionSpec as P

MESH = pl.DeviceIdType.MESH
F32 = jnp.float32
BF16 = jnp.bfloat16
HIGH = lax.Precision.HIGHEST
PLANS = 3
STEPS = 4


def flip(bit):
    return 1 - bit


def differ(one, other):
    return (one + other) % 2


def ring_bits(place):
    high = place // 2
    return (place + high) % 2, high


def ring_place(low, high):
    return 2 * high + (low + high) % 2


def blk_bits(index):
    low, high = ring_bits(index % 4)
    return low, high, index // 4


def blk_index(bits):
    return bits[2] * 4 + ring_place(bits[0], bits[1])


def weigh(mine, assign, orders, offsets, row_weight, coupling, right):
    n_rows = right.shape[0]
    n_blocks = assign.shape[0]
    slots = lax.broadcasted_iota(jnp.int32, (1, n_rows), 1)
    members, scaled = [], []
    for block in range(n_blocks):
        start = offsets[block]
        inside = (
            (jnp.full((1, n_rows), assign[block], jnp.int32) == mine)
            & (slots >= start)
            & (slots < start + orders[block])
        ).astype(F32)
        members.append(inside)
        scaled.append(inside / jnp.sqrt(jnp.full((1, n_rows), orders[block], jnp.int32).astype(F32)))
    member = jnp.concatenate(members, axis=0)
    shares = jnp.concatenate(scaled, axis=0)
    right_t = right[...].astype(F32).T
    sums = lax.dot_general(
        right_t * coupling[...], member, (((1,), (1,)), ((), ())), precision=HIGH, preferred_element_type=F32
    )
    spread = lax.dot_general(
        sums, shares, (((1,), (0,)), ((), ())), precision=HIGH, preferred_element_type=F32
    )
    live = jnp.sum(member, axis=0, keepdims=True)
    return (live * row_weight[...] * right_t + coupling[...] * spread).astype(BF16)


def kernel(
    assign, orders, offsets, row_weight, coupling, right, left, out,
    slabs, weights, piece, partial, arrived, total, final,
    own_send, own_recv, fwd_send, fwd_recv, sum_send, sum_recv,
    local_sem, put_send, put_recv, x_send, x_recv, xf_send, xf_recv, core_send, core_recv, out_sem,
):
    height, width = left.shape
    plan_width = width // PLANS
    step_width = plan_width // STEPS
    half = height // 2
    block = weights.shape[2]
    core_rows = block // 2
    x_rows = core_rows // 4
    blk = lax.axis_index("blk")
    tile = lax.axis_index("tile")
    x, z_hi, core = tile // 4, (tile // 2) % 2, tile % 2
    bits = blk_bits(blk)
    x_bits = ring_bits(x)

    def across(dim):
        return blk_index([flip(bit) if at == dim else bit for at, bit in enumerate(bits)])

    def beside(dim):
        place = ring_place(*[flip(bit) if at == dim else bit for at, bit in enumerate(x_bits)])
        return place * 4 + z_hi * 2 + core

    def remote(src, dst, send, recv, blk_to, tile_to):
        return pltpu.make_async_remote_copy(
            src_ref=src, dst_ref=dst, send_sem=send, recv_sem=recv,
            device_id=(blk_to, tile_to), device_id_type=MESH,
        )

    def columns(plan, step):
        return pl.ds(pl.multiple_of(plan * plan_width + step * step_width, step_width), step_width)

    def own_copy(plan, step, side):
        cols = columns(plan, step)
        return remote(
            left.at[:, cols], slabs.at[1 + side, :, cols],
            own_send.at[plan, step, side], own_recv.at[plan, step, side],
            across((plan + 1 + side) % 3), tile,
        )

    def fwd_copy(plan, step, side):
        cols = columns(plan, step)
        rows = pl.ds(side * half, half)
        return remote(
            slabs.at[2 - side, rows, cols], slabs.at[3, rows, cols],
            fwd_send.at[plan, step, side], fwd_recv.at[plan, step, side],
            across((plan + 1 + side) % 3), tile,
        )

    def sum_copy(plan, step):
        cols = columns(plan, step)
        return remote(
            partial.at[:, cols], arrived.at[:, cols],
            sum_send.at[plan, step], sum_recv.at[plan, step], across(plan), tile,
        )

    local = pltpu.make_async_copy(left, slabs.at[0], local_sem)
    local.start()

    def send_own(step):
        for plan in range(PLANS):
            for side in range(2):
                own_copy(plan, step, side).start()

    send_own(0)

    piece[...] = weigh(blk, assign, orders, offsets, row_weight, coupling, right)
    band_bits = blk_bits(2 * x + z_hi)

    def put(plan):
        q, r = (plan + 1) % 3, (plan + 2) % 3
        goal = blk_index([bits[at] if at == plan else band_bits[at] for at in range(3)])
        kind = differ(band_bits[plan], bits[plan])
        slot = differ(band_bits[q], bits[q]) + 2 * differ(band_bits[r], bits[r])
        lanes = pl.ds(pl.multiple_of(slot * height, height), height)
        for x_to in range(4):
            for z_to in range(2):
                goal_tile = x_to * 4 + z_to * 2 + core
                rows = pl.ds(pl.multiple_of(core * core_rows + x_to * x_rows, x_rows), x_rows)
                src = piece.at[pl.ds(x_to * x_rows, x_rows), :]
                dst = weights.at[plan, kind, rows, lanes]
                stays = (goal == blk) & (goal_tile == tile)
                yield stays, src, dst, goal, goal_tile, put_send.at[plan, x_to, z_to], put_recv.at[plan]

    for plan in range(PLANS):
        for stays, src, dst, goal, goal_tile, send, recv in put(plan):
            @pl.when(stays)
            def _():
                pltpu.make_async_copy(src, dst, recv).start()

            @pl.when(jnp.logical_not(stays))
            def _():
                remote(src, dst, send, recv, goal, goal_tile).start()

    for step in range(1, STEPS):
        send_own(step)

    def x_region(plan, x_from, first, count):
        start = pl.multiple_of(core * core_rows + x_from * x_rows + first, count)
        return weights.at[plan, :, pl.ds(start, count), :]

    x_near = [ring_place(flip(x_bits[0]), x_bits[1]), ring_place(x_bits[0], flip(x_bits[1]))]
    x_far = ring_place(flip(x_bits[0]), flip(x_bits[1]))

    def x_copy(plan, side):
        region = x_region(plan, x, 0, x_rows)
        return remote(region, region, x_send.at[plan, side], x_recv.at[plan, side], blk, beside(side))

    def xf_copy(plan, side):
        region = x_region(plan, x_near[1 - side], side * (x_rows // 2), x_rows // 2)
        return remote(region, region, xf_send.at[plan, side], xf_recv.at[plan, side], blk, beside(side))

    def core_copy(plan, index, x_from):
        region = x_region(plan, x_from, 0, x_rows)
        return remote(
            region, region, core_send.at[plan, index], core_recv.at[plan, index], blk, tile + 1 - 2 * core
        )

    order = [x, x_near[0], x_near[1], x_far]
    for plan in range(PLANS):
        region = x_region(plan, x, 0, x_rows)
        pltpu.make_async_copy(region, region, put_recv.at[plan]).wait()
        for side in range(2):
            x_copy(plan, side).start()
        core_copy(plan, 0, order[0]).start()

    def forward(step):
        for plan in range(PLANS):
            for side in range(2):
                own_copy(plan, step, side).wait_recv()
            for side in range(2):
                fwd_copy(plan, step, side).start()

    forward(0)
    for plan in range(PLANS):
        for side in range(2):
            x_copy(plan, side).wait_recv()
        for side in range(2):
            xf_copy(plan, side).start()
        for side in range(2):
            core_copy(plan, 1 + side, order[1 + side]).start()
    for step in range(1, STEPS):
        forward(step)
    for plan in range(PLANS):
        for side in range(2):
            xf_copy(plan, side).wait_recv()
        core_copy(plan, 3, order[3]).start()
    for plan in range(PLANS):
        for index in range(4):
            core_copy(plan, index, order[index]).wait_recv()
    local.wait()

    def product(plan, kind, cols):
        rows = slabs[:, :, cols].reshape(4 * height, step_width)
        return jnp.dot(weights[plan, kind], rows, preferred_element_type=F32)

    @pl.loop(0, STEPS)
    def _(step):
        for plan in range(PLANS):
            cols = columns(plan, step)
            for side in range(2):
                fwd_copy(plan, step, side).wait_recv()
            partial[:, cols] = product(plan, 1, cols).astype(BF16)
            sum_copy(plan, step).start()
        for plan in range(PLANS):
            cols = columns(plan, step)
            total[:, cols] = product(plan, 0, cols)

    def out_copy(plan, step):
        cols = columns(plan, step)
        return pltpu.make_async_copy(final.at[:, cols], out.at[:, cols], out_sem.at[plan, step])

    @pl.loop(0, STEPS)
    def _(step):
        for plan in range(PLANS):
            cols = columns(plan, step)
            sum_copy(plan, step).wait_recv()
            final[:, cols] = (total[:, cols] + arrived[:, cols].astype(F32)).astype(BF16)
            out_copy(plan, step).start()

    for plan in range(PLANS):
        for stays, src, dst, goal, goal_tile, send, recv in put(plan):
            @pl.when(jnp.logical_not(stays))
            def _():
                remote(src, dst, send, recv, goal, goal_tile).wait_send()
        for side in range(2):
            x_copy(plan, side).wait_send()
            xf_copy(plan, side).wait_send()
        for index in range(4):
            core_copy(plan, index, order[index]).wait_send()

    @pl.loop(0, STEPS)
    def _(step):
        for plan in range(PLANS):
            for side in range(2):
                own_copy(plan, step, side).wait_send()
                fwd_copy(plan, step, side).wait_send()
            sum_copy(plan, step).wait_send()
            out_copy(plan, step).wait()


def shards(left_rows, right_rows, row_weight, coupling, assign, orders, offsets):
    height, width = left_rows.shape
    band = right_rows.shape[1] * lax.axis_size("tile")
    block = band // lax.axis_size("blk")
    dma = pltpu.SemaphoreType.DMA
    smem = pl.BlockSpec(memory_space=pltpu.SMEM)
    vmem = pl.BlockSpec(memory_space=pltpu.VMEM)
    hbm = pl.BlockSpec(memory_space=pl.ANY)
    return pl.pallas_call(
        kernel,
        out_shape=jax.ShapeDtypeStruct((block, width), BF16),
        in_specs=[smem, smem, smem, vmem, vmem, vmem, hbm],
        out_specs=hbm,
        scratch_shapes=[
            pltpu.VMEM((4, height, width), BF16),
            pltpu.VMEM((PLANS, 2, block, 4 * height), BF16),
            pltpu.VMEM((right_rows.shape[1], height), BF16),
            pltpu.VMEM((block, width), BF16),
            pltpu.VMEM((block, width), BF16),
            pltpu.VMEM((block, width), F32),
            pltpu.VMEM((block, width), BF16),
            dma((PLANS, STEPS, 2)), dma((PLANS, STEPS, 2)),
            dma((PLANS, STEPS, 2)), dma((PLANS, STEPS, 2)),
            dma((PLANS, STEPS)), dma((PLANS, STEPS)),
            dma, dma((PLANS, 4, 2)), dma((PLANS,)),
            dma((PLANS, 2)), dma((PLANS, 2)),
            dma((PLANS, 2)), dma((PLANS, 2)),
            dma((PLANS, 4)), dma((PLANS, 4)),
            dma((PLANS, STEPS)),
        ],
        compiler_params=pltpu.CompilerParams(has_side_effects=True, vmem_limit_bytes=60 * 2**20),
    )(
        assign, orders, offsets, row_weight.reshape(1, height), coupling.reshape(1, height), right_rows, left_rows
    )


def solution(mesh):
    return jax.shard_map(
        shards,
        mesh=mesh,
        in_specs=(P("blk", "tile"), P("blk", "tile"), P("blk"), P("blk"), P(), P(), P()),
        out_specs=P("blk", "tile"),
        check_vma=False,
    )
```

```python
import functools

import jax
import jax.numpy as jnp
from jax import lax
from jax.experimental import pallas as pl
from jax.experimental.pallas import tpu as pltpu
from jax.sharding import PartitionSpec as P

MESH = pl.DeviceIdType.MESH
F32 = jnp.float32
BF16 = jnp.bfloat16
HIGH = lax.Precision.HIGHEST
PLANS = 3
STEPS = 4


def flip(bit):
    return 1 - bit


def differ(one, other):
    return (one + other) % 2


def ring_bits(place):
    high = place // 2
    return (place + high) % 2, high


def ring_place(low, high):
    return 2 * high + (low + high) % 2


def blk_bits(index):
    low, high = ring_bits(index % 4)
    return low, high, index // 4


def blk_index(bits):
    return bits[2] * 4 + ring_place(bits[0], bits[1])


def weigh(mine, assign, orders, offsets, row_weight, coupling, right):
    n_rows = right.shape[0]
    n_blocks = assign.shape[0]
    slots = lax.broadcasted_iota(jnp.int32, (1, n_rows), 1)
    members, scaled = [], []
    for block in range(n_blocks):
        start = offsets[block]
        inside = (
            (jnp.full((1, n_rows), assign[block], jnp.int32) == mine)
            & (slots >= start)
            & (slots < start + orders[block])
        ).astype(F32)
        members.append(inside)
        scaled.append(inside / jnp.sqrt(jnp.full((1, n_rows), orders[block], jnp.int32).astype(F32)))
    member = jnp.concatenate(members, axis=0)
    shares = jnp.concatenate(scaled, axis=0)
    right_t = right[...].astype(F32).T
    sums = lax.dot_general(
        right_t * coupling[...], member, (((1,), (1,)), ((), ())), precision=HIGH, preferred_element_type=F32
    )
    spread = lax.dot_general(
        sums, shares, (((1,), (0,)), ((), ())), precision=HIGH, preferred_element_type=F32
    )
    live = jnp.sum(member, axis=0, keepdims=True)
    return (live * row_weight[...] * right_t + coupling[...] * spread).astype(BF16)


def kernel(
    assign, orders, offsets, row_weight, coupling, right, left, out,
    slabs, weights, piece, quarters, partial, arrived, total,
    own_send, own_recv, fwd_send, fwd_recv, sum_send, sum_recv,
    local_sem, part_send, part_recv, z_send, z_recv, zf_send, zf_recv, put_send, put_recv,
    x_send, x_recv, xf_send, xf_recv, core_send, core_recv,
):
    height, width = left.shape
    plan_width = width // PLANS
    step_width = plan_width // STEPS
    half = height // 2
    block = weights.shape[2]
    core_rows = block // 2
    x_rows = core_rows // 4
    blk = lax.axis_index("blk")
    tile = lax.axis_index("tile")
    x, z_hi, core = tile // 4, (tile // 2) % 2, tile % 2
    y, z = blk % 4, z_hi * 2 + blk // 4
    bits = blk_bits(blk)
    x_bits, z_bits = ring_bits(x), ring_bits(z)

    def device(x_to, y_to, z_to, core_to):
        return (z_to % 2) * 4 + y_to, x_to * 4 + (z_to // 2) * 2 + core_to

    def across(dim):
        return blk_index([flip(bit) if at == dim else bit for at, bit in enumerate(bits)]), tile

    def moved(place_bits, *flips):
        return ring_place(*[differ(bit, by) for bit, by in zip(place_bits, flips)])

    x_near = [moved(x_bits, 1, 0), moved(x_bits, 0, 1)]
    x_far = moved(x_bits, 1, 1)
    z_near = [moved(z_bits, 1, 0), moved(z_bits, 0, 1)]
    y_bits = bits[:2]
    x_peers = [device(to, y, z, core) for to in (*x_near, x_far)]
    z_peers = [device(x, y, to, core) for to in z_near]
    y_peers = {by: device(x, moved(y_bits, *by), z, core) for by in ((1, 0), (0, 1), (1, 1))}
    twin = device(x, y, z, 1 - core)

    barrier = pltpu.get_barrier_semaphore()
    peers = [*y_peers.values(), *z_peers, *x_peers, twin]
    for peer in peers:
        pl.semaphore_signal(barrier, inc=1, device_id=peer, device_id_type=MESH)
    pl.semaphore_wait(barrier, len(peers))

    def remote(src, dst, send, recv, peer):
        return pltpu.make_async_remote_copy(
            src_ref=src, dst_ref=dst, send_sem=send, recv_sem=recv,
            device_id=peer, device_id_type=MESH,
        )

    def columns(plan, step):
        return pl.ds(pl.multiple_of(plan * plan_width + step * step_width, step_width), step_width)

    def own_copy(plan, step, side):
        cols = columns(plan, step)
        return remote(
            left.at[:, cols], slabs.at[1 + side, :, cols],
            own_send.at[plan, step, side], own_recv.at[plan, step, side],
            across((plan + 1 + side) % 3),
        )

    def fwd_copy(plan, step, side):
        cols = columns(plan, step)
        rows = pl.ds(side * half, half)
        return remote(
            slabs.at[2 - side, rows, cols], slabs.at[3, rows, cols],
            fwd_send.at[plan, step, side], fwd_recv.at[plan, step, side],
            across((plan + 1 + side) % 3),
        )

    def sum_copy(plan, step):
        cols = columns(plan, step)
        return remote(
            partial.at[:, cols], arrived.at[:, cols],
            sum_send.at[plan, step], sum_recv.at[plan, step], across(plan),
        )

    local = pltpu.make_async_copy(left, slabs.at[0], local_sem.at[0])
    local.start()

    def send_own(step):
        for plan in range(PLANS):
            for side in range(2):
                own_copy(plan, step, side).start()

    send_own(0)

    piece[...] = weigh(blk, assign, orders, offsets, row_weight, coupling, right)

    def quarter(index):
        return piece.at[pl.ds(pl.multiple_of(index * x_rows, x_rows), x_rows), :]

    def part_copy(index):
        place = (*x_near, x_far)[index]
        return remote(
            quarter(place), quarters.at[z, x], part_send.at[index], part_recv.at[index], x_peers[index]
        )

    kept = pltpu.make_async_copy(quarter(x), quarters.at[z, x], local_sem.at[1])
    for index in range(3):
        part_copy(index).start()
    kept.start()

    def z_copy(side):
        return remote(quarters.at[z], quarters.at[z], z_send.at[side], z_recv.at[side], z_peers[side])

    def zf_copy(side):
        part = quarters.at[z_near[1 - side], pl.ds(2 * side, 2)]
        return remote(part, part, zf_send.at[side], zf_recv.at[side], z_peers[side])

    kept.wait()
    for index in range(3):
        part_copy(index).wait_recv()
    for side in range(2):
        z_copy(side).start()

    plane = bits[2]

    def puts(plan):
        for first in range(2):
            for second in range(2):
                if plan < 2:
                    for far in range(2):
                        from_bit, to_bit = first, second
                        own, over = bits[plan], bits[1 - plan]
                        band = [None, None]
                        band[plan], band[1 - plan] = differ(own, from_bit), differ(over, far)
                        slab_plane = to_bit
                        spots = [None, None]
                        spots[plan], spots[1 - plan] = 0, far
                        apart = differ(slab_plane, plane)
                        slot = apart + 2 * far if plan == 1 else far + 2 * apart
                        yield tuple(spots), slab_plane, band, plane, from_bit, slot
                else:
                    for band_plane in range(2):
                        band = [differ(bits[0], first), differ(bits[1], second)]
                        yield (first, second), plane, band, band_plane, differ(band_plane, plane), first + 2 * second

    def x_region(plan, x_from, first, count):
        start = pl.multiple_of(core * core_rows + x_from * x_rows + first, count)
        return weights.at[plan, :, pl.ds(start, count), :]

    def put_copies(plan, with_local):
        for index, (move, slab_plane, band, band_plane, kind, slot) in enumerate(puts(plan)):
            band_z_hi = differ(band[0], band[1])
            band_x = 2 * band_plane + band[1]
            rows = pl.ds(pl.multiple_of(core * core_rows + x * x_rows, x_rows), x_rows)
            lanes = pl.ds(pl.multiple_of(slot * height, height), height)
            src = quarters.at[band_z_hi * 2 + slab_plane, band_x]
            dst = weights.at[plan, kind, rows, lanes]
            if move != (0, 0):
                yield remote(src, dst, put_send.at[plan, index], put_recv.at[plan], y_peers[move])
            elif with_local:
                yield pltpu.make_async_copy(src, dst, put_recv.at[plan])

    def x_copy(plan, side):
        region = x_region(plan, x, 0, x_rows)
        return remote(region, region, x_send.at[plan, side], x_recv.at[plan, side], x_peers[side])

    def xf_copy(plan, side):
        region = x_region(plan, x_near[1 - side], side * (x_rows // 2), x_rows // 2)
        return remote(region, region, xf_send.at[plan, side], xf_recv.at[plan, side], x_peers[side])

    def core_copy(plan, index):
        region = x_region(plan, (x, *x_near, x_far)[index], 0, x_rows)
        return remote(region, region, core_send.at[plan, index], core_recv.at[plan, index], twin)

    def forward(step):
        for plan in range(PLANS):
            for side in range(2):
                own_copy(plan, step, side).wait_recv()
            for side in range(2):
                fwd_copy(plan, step, side).start()

    send_own(1)
    for side in range(2):
        z_copy(side).wait_recv()
    for side in range(2):
        zf_copy(side).start()
    send_own(2)
    forward(0)
    for side in range(2):
        zf_copy(side).wait_recv()
    for plan in range(PLANS):
        for copy in put_copies(plan, True):
            copy.start()
    send_own(3)
    forward(1)
    for plan in range(PLANS):
        region = x_region(plan, x, 0, x_rows)
        pltpu.make_async_copy(region, region, put_recv.at[plan]).wait()
        for side in range(2):
            x_copy(plan, side).start()
        core_copy(plan, 0).start()
    forward(2)
    for plan in range(PLANS):
        for side in range(2):
            x_copy(plan, side).wait_recv()
        for side in range(2):
            xf_copy(plan, side).start()
        for index in (1, 2):
            core_copy(plan, index).start()
    forward(3)
    for plan in range(PLANS):
        for side in range(2):
            xf_copy(plan, side).wait_recv()
        core_copy(plan, 3).start()
    for plan in range(PLANS):
        for index in range(4):
            core_copy(plan, index).wait_recv()
    local.wait()

    def product(plan, kind, cols):
        rows = slabs[:, :, cols].reshape(4 * height, step_width)
        return jnp.dot(weights[plan, kind], rows, preferred_element_type=F32)

    @pl.loop(0, STEPS)
    def _(step):
        for plan in range(PLANS):
            cols = columns(plan, step)
            for side in range(2):
                fwd_copy(plan, step, side).wait_recv()
            partial[:, cols] = product(plan, 1, cols).astype(BF16)
            sum_copy(plan, step).start()
        for plan in range(PLANS):
            cols = columns(plan, step)
            total[:, cols] = product(plan, 0, cols)

    @pl.loop(0, STEPS)
    def _(step):
        for plan in range(PLANS):
            cols = columns(plan, step)
            sum_copy(plan, step).wait_recv()
            out[:, cols] = (total[:, cols] + arrived[:, cols].astype(F32)).astype(BF16)

    for index in range(3):
        part_copy(index).wait_send()
    for side in range(2):
        z_copy(side).wait_send()
        zf_copy(side).wait_send()
    for plan in range(PLANS):
        for copy in put_copies(plan, False):
            copy.wait_send()
        for side in range(2):
            x_copy(plan, side).wait_send()
            xf_copy(plan, side).wait_send()
        for index in range(4):
            core_copy(plan, index).wait_send()

    @pl.loop(0, STEPS)
    def _(step):
        for plan in range(PLANS):
            for side in range(2):
                own_copy(plan, step, side).wait_send()
                fwd_copy(plan, step, side).wait_send()
            sum_copy(plan, step).wait_send()


def shards(left_rows, right_rows, row_weight, coupling, assign, orders, offsets):
    height, width = left_rows.shape
    band = right_rows.shape[1] * lax.axis_size("tile")
    block = band // lax.axis_size("blk")
    dma = pltpu.SemaphoreType.DMA
    smem = pl.BlockSpec(memory_space=pltpu.SMEM)
    vmem = pl.BlockSpec(memory_space=pltpu.VMEM)
    hbm = pl.BlockSpec(memory_space=pl.ANY)
    return pl.pallas_call(
        kernel,
        out_shape=pltpu.VMEM((block, width), BF16),
        in_specs=[smem, smem, smem, vmem, vmem, vmem, hbm],
        out_specs=vmem,
        scratch_shapes=[
            pltpu.VMEM((4, height, width), BF16),
            pltpu.VMEM((PLANS, 2, block, 4 * height), BF16),
            pltpu.VMEM((right_rows.shape[1], height), BF16),
            pltpu.VMEM((4, 4, right_rows.shape[1] // 4, height), BF16),
            pltpu.VMEM((block, width), BF16),
            pltpu.VMEM((block, width), BF16),
            pltpu.VMEM((block, width), F32),
            dma((PLANS, STEPS, 2)), dma((PLANS, STEPS, 2)),
            dma((PLANS, STEPS, 2)), dma((PLANS, STEPS, 2)),
            dma((PLANS, STEPS)), dma((PLANS, STEPS)),
            dma((2,)), dma((3,)), dma((3,)), dma((2,)), dma((2,)), dma((2,)), dma((2,)),
            dma((PLANS, 8)), dma((PLANS,)),
            dma((PLANS, 2)), dma((PLANS, 2)),
            dma((PLANS, 2)), dma((PLANS, 2)),
            dma((PLANS, 4)), dma((PLANS, 4)),
        ],
        compiler_params=pltpu.CompilerParams(collective_id=0, has_side_effects=True, vmem_limit_bytes=60 * 2**20),
    )(
        assign, orders, offsets, row_weight.reshape(1, height), coupling.reshape(1, height), right_rows, left_rows
    )


def solution(mesh):
    return jax.shard_map(
        shards,
        mesh=mesh,
        in_specs=(P("blk", "tile"), P("blk", "tile"), P("blk"), P("blk"), P(), P(), P()),
        out_specs=P("blk", "tile"),
        check_vma=False,
    )
```

```python
import functools

import jax
import jax.numpy as jnp
from jax import lax
from jax.experimental import pallas as pl
from jax.experimental.pallas import tpu as pltpu
from jax.sharding import PartitionSpec as P

MESH = pl.DeviceIdType.MESH
F32 = jnp.float32
BF16 = jnp.bfloat16
HIGH = lax.Precision.HIGHEST
PLANS = 3
STEPS = 4


def flip(bit):
    return 1 - bit


def differ(one, other):
    return (one + other) % 2


def ring_bits(place):
    high = place // 2
    return (place + high) % 2, high


def ring_place(low, high):
    return 2 * high + (low + high) % 2


def blk_bits(index):
    low, high = ring_bits(index % 4)
    return low, high, index // 4


def blk_index(bits):
    return bits[2] * 4 + ring_place(bits[0], bits[1])


def weigh(mine, assign, orders, offsets, row_weight, coupling, right):
    n_rows = right.shape[0]
    n_blocks = assign.shape[0]
    slots = lax.broadcasted_iota(jnp.int32, (1, n_rows), 1)
    members, scaled = [], []
    for block in range(n_blocks):
        start = offsets[block]
        inside = (
            (jnp.full((1, n_rows), assign[block], jnp.int32) == mine)
            & (slots >= start)
            & (slots < start + orders[block])
        ).astype(F32)
        members.append(inside)
        scaled.append(inside / jnp.sqrt(jnp.full((1, n_rows), orders[block], jnp.int32).astype(F32)))
    member = jnp.concatenate(members, axis=0)
    shares = jnp.concatenate(scaled, axis=0)
    right_t = right[...].astype(F32).T
    sums = lax.dot_general(
        right_t * coupling[...], member, (((1,), (1,)), ((), ())), precision=HIGH, preferred_element_type=F32
    )
    spread = lax.dot_general(
        sums, shares, (((1,), (0,)), ((), ())), precision=HIGH, preferred_element_type=F32
    )
    live = jnp.sum(member, axis=0, keepdims=True)
    return (live * row_weight[...] * right_t + coupling[...] * spread).astype(BF16)


def kernel(
    assign, orders, offsets, row_weight, coupling, right, left, out,
    slabs, weights, piece, quarters, partial, arrived, total,
    own_send, own_recv, fwd_send, fwd_recv, sum_send, sum_recv,
    local_sem, part_send, part_recv, z_send, z_recv, zf_send, zf_recv, put_send, put_recv,
    x_send, x_recv, xf_send, xf_recv, core_send, core_recv,
):
    height, width = left.shape
    plan_width = width // PLANS
    step_width = plan_width // STEPS
    half = height // 2
    block = weights.shape[2]
    core_rows = block // 2
    x_rows = core_rows // 4
    blk = lax.axis_index("blk")
    tile = lax.axis_index("tile")
    x, z_hi, core = tile // 4, (tile // 2) % 2, tile % 2
    y, z = blk % 4, z_hi * 2 + blk // 4
    bits = blk_bits(blk)
    x_bits, z_bits = ring_bits(x), ring_bits(z)

    def device(x_to, y_to, z_to, core_to):
        return (z_to % 2) * 4 + y_to, x_to * 4 + (z_to // 2) * 2 + core_to

    def across(dim):
        return blk_index([flip(bit) if at == dim else bit for at, bit in enumerate(bits)]), tile

    def moved(place_bits, *flips):
        return ring_place(*[differ(bit, by) for bit, by in zip(place_bits, flips)])

    x_near = [moved(x_bits, 1, 0), moved(x_bits, 0, 1)]
    x_far = moved(x_bits, 1, 1)
    z_near = [moved(z_bits, 1, 0), moved(z_bits, 0, 1)]
    y_bits = bits[:2]
    x_peers = [device(to, y, z, core) for to in (*x_near, x_far)]
    z_peers = [device(x, y, to, core) for to in z_near]
    y_peers = {by: device(x, moved(y_bits, *by), z, core) for by in ((1, 0), (0, 1), (1, 1))}
    twin = device(x, y, z, 1 - core)

    barrier = pltpu.get_barrier_semaphore()
    peers = [*y_peers.values(), *z_peers, *x_peers, twin]
    for peer in peers:
        pl.semaphore_signal(barrier, inc=1, device_id=peer, device_id_type=MESH)
    pl.semaphore_wait(barrier, len(peers))

    def remote(src, dst, send, recv, peer):
        return pltpu.make_async_remote_copy(
            src_ref=src, dst_ref=dst, send_sem=send, recv_sem=recv,
            device_id=peer, device_id_type=MESH,
        )

    def columns(plan, step):
        return pl.ds(pl.multiple_of(plan * plan_width + step * step_width, step_width), step_width)

    def own_copy(plan, step, side):
        cols = columns(plan, step)
        return remote(
            left.at[:, cols], slabs.at[1 + side, :, cols],
            own_send.at[plan, step, side], own_recv.at[plan, step, side],
            across((plan + 1 + side) % 3),
        )

    def fwd_copy(plan, step, side):
        cols = columns(plan, step)
        rows = pl.ds(side * half, half)
        return remote(
            slabs.at[2 - side, rows, cols], slabs.at[3, rows, cols],
            fwd_send.at[plan, step, side], fwd_recv.at[plan, step, side],
            across((plan + 1 + side) % 3),
        )

    def sum_copy(plan, step):
        cols = columns(plan, step)
        return remote(
            partial.at[:, cols], arrived.at[:, cols],
            sum_send.at[plan, step], sum_recv.at[plan, step], across(plan),
        )

    local = pltpu.make_async_copy(left, slabs.at[0], local_sem.at[0])
    local.start()

    def send_own(step):
        for plan in range(PLANS):
            for side in range(2):
                own_copy(plan, step, side).start()

    send_own(0)

    piece[...] = weigh(blk, assign, orders, offsets, row_weight, coupling, right)

    def quarter(index):
        return piece.at[pl.ds(pl.multiple_of(index * x_rows, x_rows), x_rows), :]

    def part_copy(index):
        place = (*x_near, x_far)[index]
        return remote(
            quarter(place), quarters.at[z, x], part_send.at[index], part_recv.at[index], x_peers[index]
        )

    kept = pltpu.make_async_copy(quarter(x), quarters.at[z, x], local_sem.at[1])
    for index in range(3):
        part_copy(index).start()
    kept.start()

    def z_copy(side):
        return remote(quarters.at[z], quarters.at[z], z_send.at[side], z_recv.at[side], z_peers[side])

    def zf_copy(side):
        part = quarters.at[z_near[1 - side], pl.ds(2 * side, 2)]
        return remote(part, part, zf_send.at[side], zf_recv.at[side], z_peers[side])

    kept.wait()
    for index in range(3):
        part_copy(index).wait_recv()
    for side in range(2):
        z_copy(side).start()

    plane = bits[2]

    def puts(plan, kind):
        for first in range(2):
            for second in range(2):
                if plan < 2:
                    far, slab_plane = first, second
                    band, move = [None, None], [None, None]
                    band[plan], band[1 - plan] = differ(bits[plan], kind), differ(bits[1 - plan], far)
                    move[plan], move[1 - plan] = 0, far
                    apart = differ(slab_plane, plane)
                    slot = apart + 2 * far if plan == 1 else far + 2 * apart
                    yield tuple(move), slab_plane, band, plane, kind, slot
                else:
                    band = [differ(bits[0], first), differ(bits[1], second)]
                    yield (first, second), plane, band, differ(plane, kind), kind, first + 2 * second

    def x_region(plan, kind, x_from, first, count):
        start = pl.multiple_of(core * core_rows + x_from * x_rows + first, count)
        return weights.at[plan, kind, pl.ds(start, count), :]

    def put_copies(plan, kind_now, with_local):
        for index, (move, slab_plane, band, band_plane, kind, slot) in enumerate(puts(plan, kind_now)):
            band_z_hi = differ(band[0], band[1])
            band_x = 2 * band_plane + band[1]
            rows = pl.ds(pl.multiple_of(core * core_rows + x * x_rows, x_rows), x_rows)
            lanes = pl.ds(pl.multiple_of(slot * height, height), height)
            src = quarters.at[band_z_hi * 2 + slab_plane, band_x]
            dst = weights.at[plan, kind, rows, lanes]
            if move != (0, 0):
                yield remote(src, dst, put_send.at[plan, kind, index], put_recv.at[plan, kind], y_peers[move])
            elif with_local:
                yield pltpu.make_async_copy(src, dst, put_recv.at[plan, kind])

    def x_copy(plan, kind, side):
        region = x_region(plan, kind, x, 0, x_rows)
        return remote(region, region, x_send.at[plan, kind, side], x_recv.at[plan, kind, side], x_peers[side])

    def xf_copy(plan, kind, side):
        region = x_region(plan, kind, x_near[1 - side], side * (x_rows // 2), x_rows // 2)
        return remote(region, region, xf_send.at[plan, kind, side], xf_recv.at[plan, kind, side], x_peers[side])

    def core_copy(plan, kind, index):
        region = x_region(plan, kind, (x, *x_near, x_far)[index], 0, x_rows)
        return remote(region, region, core_send.at[plan, kind, index], core_recv.at[plan, kind, index], twin)

    def x_begin(plan, kind):
        region = x_region(plan, kind, x, 0, x_rows)
        pltpu.make_async_copy(region, region, put_recv.at[plan, kind]).wait()
        for side in range(2):
            x_copy(plan, kind, side).start()
        core_copy(plan, kind, 0).start()

    def x_pass(plan, kind):
        for side in range(2):
            x_copy(plan, kind, side).wait_recv()
        for side in range(2):
            xf_copy(plan, kind, side).start()
        for index in (1, 2):
            core_copy(plan, kind, index).start()

    def x_end(plan, kind):
        for side in range(2):
            xf_copy(plan, kind, side).wait_recv()
        core_copy(plan, kind, 3).start()

    def core_end(plan, kind):
        for index in range(4):
            core_copy(plan, kind, index).wait_recv()

    def forward(step):
        for plan in range(PLANS):
            for side in range(2):
                own_copy(plan, step, side).wait_recv()
            for side in range(2):
                fwd_copy(plan, step, side).start()

    send_own(1)
    for side in range(2):
        z_copy(side).wait_recv()
    for side in range(2):
        zf_copy(side).start()
    send_own(2)
    forward(0)
    for side in range(2):
        zf_copy(side).wait_recv()
    for kind in (1, 0):
        for plan in range(PLANS):
            for copy in put_copies(plan, kind, True):
                copy.start()
        if kind == 1:
            send_own(3)
            forward(1)
    for plan in range(PLANS):
        x_begin(plan, 1)
    forward(2)
    for plan in range(PLANS):
        x_pass(plan, 1)
    for plan in range(PLANS):
        x_begin(plan, 0)
    forward(3)
    for plan in range(PLANS):
        x_end(plan, 1)
    for plan in range(PLANS):
        core_end(plan, 1)
    local.wait()

    def product(plan, kind, cols):
        rows = slabs[:, :, cols].reshape(4 * height, step_width)
        return jnp.dot(weights[plan, kind], rows, preferred_element_type=F32)

    @pl.loop(0, STEPS)
    def _(step):
        for plan in range(PLANS):
            cols = columns(plan, step)
            for side in range(2):
                fwd_copy(plan, step, side).wait_recv()
            partial[:, cols] = product(plan, 1, cols).astype(BF16)
            sum_copy(plan, step).start()

    for stage in (x_pass, x_end, core_end):
        for plan in range(PLANS):
            stage(plan, 0)

    @pl.loop(0, STEPS)
    def _(step):
        for plan in range(PLANS):
            cols = columns(plan, step)
            total[:, cols] = product(plan, 0, cols)

    @pl.loop(0, STEPS)
    def _(step):
        for plan in range(PLANS):
            cols = columns(plan, step)
            sum_copy(plan, step).wait_recv()
            out[:, cols] = (total[:, cols] + arrived[:, cols].astype(F32)).astype(BF16)

    for index in range(3):
        part_copy(index).wait_send()
    for side in range(2):
        z_copy(side).wait_send()
        zf_copy(side).wait_send()
    for plan in range(PLANS):
        for kind in range(2):
            for copy in put_copies(plan, kind, False):
                copy.wait_send()
            for side in range(2):
                x_copy(plan, kind, side).wait_send()
                xf_copy(plan, kind, side).wait_send()
            for index in range(4):
                core_copy(plan, kind, index).wait_send()

    @pl.loop(0, STEPS)
    def _(step):
        for plan in range(PLANS):
            for side in range(2):
                own_copy(plan, step, side).wait_send()
                fwd_copy(plan, step, side).wait_send()
            sum_copy(plan, step).wait_send()


def shards(left_rows, right_rows, row_weight, coupling, assign, orders, offsets):
    height, width = left_rows.shape
    band = right_rows.shape[1] * lax.axis_size("tile")
    block = band // lax.axis_size("blk")
    dma = pltpu.SemaphoreType.DMA
    smem = pl.BlockSpec(memory_space=pltpu.SMEM)
    vmem = pl.BlockSpec(memory_space=pltpu.VMEM)
    hbm = pl.BlockSpec(memory_space=pl.ANY)
    return pl.pallas_call(
        kernel,
        out_shape=pltpu.VMEM((block, width), BF16),
        in_specs=[smem, smem, smem, vmem, vmem, vmem, hbm],
        out_specs=vmem,
        scratch_shapes=[
            pltpu.VMEM((4, height, width), BF16),
            pltpu.VMEM((PLANS, 2, block, 4 * height), BF16),
            pltpu.VMEM((right_rows.shape[1], height), BF16),
            pltpu.VMEM((4, 4, right_rows.shape[1] // 4, height), BF16),
            pltpu.VMEM((block, width), BF16),
            pltpu.VMEM((block, width), BF16),
            pltpu.VMEM((block, width), F32),
            dma((PLANS, STEPS, 2)), dma((PLANS, STEPS, 2)),
            dma((PLANS, STEPS, 2)), dma((PLANS, STEPS, 2)),
            dma((PLANS, STEPS)), dma((PLANS, STEPS)),
            dma((2,)), dma((3,)), dma((3,)), dma((2,)), dma((2,)), dma((2,)), dma((2,)),
            dma((PLANS, 2, 4)), dma((PLANS, 2)),
            dma((PLANS, 2, 2)), dma((PLANS, 2, 2)),
            dma((PLANS, 2, 2)), dma((PLANS, 2, 2)),
            dma((PLANS, 2, 4)), dma((PLANS, 2, 4)),
        ],
        compiler_params=pltpu.CompilerParams(collective_id=0, has_side_effects=True, vmem_limit_bytes=60 * 2**20),
    )(
        assign, orders, offsets, row_weight.reshape(1, height), coupling.reshape(1, height), right_rows, left_rows
    )


def solution(mesh):
    return jax.shard_map(
        shards,
        mesh=mesh,
        in_specs=(P("blk", "tile"), P("blk", "tile"), P("blk"), P("blk"), P(), P(), P()),
        out_specs=P("blk", "tile"),
        check_vma=False,
    )
```

```python
import functools

import jax
import jax.numpy as jnp
from jax import lax
from jax.experimental import pallas as pl
from jax.experimental.pallas import tpu as pltpu
from jax.sharding import PartitionSpec as P

MESH = pl.DeviceIdType.MESH
F32 = jnp.float32
BF16 = jnp.bfloat16
HIGH = lax.Precision.HIGHEST
PLANS = 3
OWN = 3
STEPS = 4


def flip(bit):
    return 1 - bit


def differ(one, other):
    return (one + other) % 2


def ring_bits(place):
    high = place // 2
    return (place + high) % 2, high


def ring_place(low, high):
    return 2 * high + (low + high) % 2


def blk_bits(index):
    low, high = ring_bits(index % 4)
    return low, high, index // 4


def blk_index(bits):
    return bits[2] * 4 + ring_place(bits[0], bits[1])


def weigh(mine, assign, orders, offsets, row_weight, coupling, right):
    n_rows = right.shape[0]
    n_blocks = assign.shape[0]
    slots = lax.broadcasted_iota(jnp.int32, (1, n_rows), 1)
    members, scaled = [], []
    for block in range(n_blocks):
        start = offsets[block]
        inside = (
            (jnp.full((1, n_rows), assign[block], jnp.int32) == mine)
            & (slots >= start)
            & (slots < start + orders[block])
        ).astype(F32)
        members.append(inside)
        scaled.append(inside / jnp.sqrt(jnp.full((1, n_rows), orders[block], jnp.int32).astype(F32)))
    member = jnp.concatenate(members, axis=0)
    shares = jnp.concatenate(scaled, axis=0)
    right_t = right[...].astype(F32).T
    sums = lax.dot_general(
        right_t * coupling[...], member, (((1,), (1,)), ((), ())), precision=HIGH, preferred_element_type=F32
    )
    spread = lax.dot_general(
        sums, shares, (((1,), (0,)), ((), ())), precision=HIGH, preferred_element_type=F32
    )
    live = jnp.sum(member, axis=0, keepdims=True)
    return (live * row_weight[...] * right_t + coupling[...] * spread).astype(BF16)


def kernel(
    assign, orders, offsets, row_weight, coupling, right, left, out,
    slabs, weights, own_weights, piece, quarters, partial, arrived, total,
    own_send, own_recv, fwd_send, fwd_recv, sum_send, sum_recv,
    local_sem, part_send, part_recv, z_send, z_recv, zf_send, zf_recv, put_send, put_recv,
    x_send, x_recv, xf_send, xf_recv, core_send, core_recv,
):
    height, width = left.shape
    plan_width = width // PLANS
    step_width = plan_width // STEPS
    half = height // 2
    block = weights.shape[1]
    core_rows = block // 2
    x_rows = core_rows // 4
    blk = lax.axis_index("blk")
    tile = lax.axis_index("tile")
    x, z_hi, core = tile // 4, (tile // 2) % 2, tile % 2
    y, z = blk % 4, z_hi * 2 + blk // 4
    bits = blk_bits(blk)
    x_bits, z_bits = ring_bits(x), ring_bits(z)

    def device(x_to, y_to, z_to, core_to):
        return (z_to % 2) * 4 + y_to, x_to * 4 + (z_to // 2) * 2 + core_to

    def across(dim):
        return blk_index([flip(bit) if at == dim else bit for at, bit in enumerate(bits)]), tile

    def moved(place_bits, *flips):
        return ring_place(*[differ(bit, by) for bit, by in zip(place_bits, flips)])

    x_near = [moved(x_bits, 1, 0), moved(x_bits, 0, 1)]
    x_far = moved(x_bits, 1, 1)
    z_near = [moved(z_bits, 1, 0), moved(z_bits, 0, 1)]
    y_bits = bits[:2]
    x_peers = [device(to, y, z, core) for to in (*x_near, x_far)]
    z_peers = [device(x, y, to, core) for to in z_near]
    y_peers = {by: device(x, moved(y_bits, *by), z, core) for by in ((1, 0), (0, 1), (1, 1))}
    twin = device(x, y, z, 1 - core)

    barrier = pltpu.get_barrier_semaphore()
    peers = [*y_peers.values(), *z_peers, *x_peers, twin]
    for peer in peers:
        pl.semaphore_signal(barrier, inc=1, device_id=peer, device_id_type=MESH)
    local = pltpu.make_async_copy(left, slabs.at[0], local_sem.at[0])
    local.start()
    piece[...] = weigh(blk, assign, orders, offsets, row_weight, coupling, right)
    pl.semaphore_wait(barrier, len(peers))

    def remote(src, dst, send, recv, peer):
        return pltpu.make_async_remote_copy(
            src_ref=src, dst_ref=dst, send_sem=send, recv_sem=recv,
            device_id=peer, device_id_type=MESH,
        )

    def columns(plan, step):
        return pl.ds(pl.multiple_of(plan * plan_width + step * step_width, step_width), step_width)

    def own_copy(plan, step, side):
        cols = columns(plan, step)
        return remote(
            left.at[:, cols], slabs.at[1 + side, :, cols],
            own_send.at[plan, step, side], own_recv.at[plan, step, side],
            across((plan + 1 + side) % 3),
        )

    def fwd_copy(plan, step, side):
        cols = columns(plan, step)
        rows = pl.ds(side * half, half)
        return remote(
            slabs.at[2 - side, rows, cols], slabs.at[3, rows, cols],
            fwd_send.at[plan, step, side], fwd_recv.at[plan, step, side],
            across((plan + 1 + side) % 3),
        )

    def sum_copy(plan, step):
        cols = columns(plan, step)
        return remote(
            partial.at[:, cols], arrived.at[:, cols],
            sum_send.at[plan, step], sum_recv.at[plan, step], across(plan),
        )

    def send_own(step, *sent):
        for plan, side in sent:
            own_copy(plan, step, side).start()

    over_y = ((0, 0), (1, 1), (2, 0), (2, 1))
    send_own(0, *over_y, (0, 1))


    def quarter(index):
        return piece.at[pl.ds(pl.multiple_of(index * x_rows, x_rows), x_rows), :]

    def part_copy(index):
        place = (*x_near, x_far)[index]
        return remote(
            quarter(place), quarters.at[z, x], part_send.at[index], part_recv.at[index], x_peers[index]
        )

    kept = pltpu.make_async_copy(quarter(x), quarters.at[z, x], local_sem.at[1])
    for index in range(3):
        part_copy(index).start()
    kept.start()

    def z_copy(side):
        return remote(quarters.at[z], quarters.at[z], z_send.at[side], z_recv.at[side], z_peers[side])

    def zf_copy(side):
        part = quarters.at[z_near[1 - side], pl.ds(2 * side, 2)]
        return remote(part, part, zf_send.at[side], zf_recv.at[side], z_peers[side])

    kept.wait()
    for index in range(3):
        part_copy(index).wait_recv()
    for side in range(2):
        z_copy(side).start()

    plane = bits[2]

    def puts(unit):
        if unit == OWN:
            for slot in range(7):
                move = (slot % 2, slot // 2 % 2)
                band = [differ(bits[0], move[0]), differ(bits[1], move[1])]
                yield move, differ(plane, slot // 4), band, plane, slot
            return
        for first in range(2):
            for second in range(2):
                if unit < 2:
                    far, slab_plane = first, second
                    band, move = [None, None], [None, None]
                    band[unit], band[1 - unit] = flip(bits[unit]), differ(bits[1 - unit], far)
                    move[unit], move[1 - unit] = 0, far
                    apart = differ(slab_plane, plane)
                    yield tuple(move), slab_plane, band, plane, apart + 2 * far if unit == 1 else far + 2 * apart
                else:
                    band = [differ(bits[0], first), differ(bits[1], second)]
                    yield (first, second), plane, band, flip(plane), first + 2 * second

    def store(unit):
        return own_weights if unit == OWN else weights.at[unit]

    def x_region(unit, x_from, first, count):
        start = pl.multiple_of(core * core_rows + x_from * x_rows + first, count)
        rows = pl.ds(start, count)
        return own_weights.at[rows, pl.ds(0, 7 * height)] if unit == OWN else weights.at[unit, rows, :]

    def put_copies(unit, with_local):
        for index, (move, slab_plane, band, band_plane, slot) in enumerate(puts(unit)):
            band_z_hi = differ(band[0], band[1])
            band_x = 2 * band_plane + band[1]
            rows = pl.ds(pl.multiple_of(core * core_rows + x * x_rows, x_rows), x_rows)
            lanes = pl.ds(pl.multiple_of(slot * height, height), height)
            src = quarters.at[band_z_hi * 2 + slab_plane, band_x]
            dst = store(unit).at[rows, lanes]
            if move != (0, 0):
                yield remote(src, dst, put_send.at[unit, index], put_recv.at[unit], y_peers[move])
            elif with_local:
                yield pltpu.make_async_copy(src, dst, put_recv.at[unit])

    def x_copy(unit, side):
        region = x_region(unit, x, 0, x_rows)
        return remote(region, region, x_send.at[unit, side], x_recv.at[unit, side], x_peers[side])

    def xf_copy(unit, side):
        region = x_region(unit, x_near[1 - side], side * (x_rows // 2), x_rows // 2)
        return remote(region, region, xf_send.at[unit, side], xf_recv.at[unit, side], x_peers[side])

    def core_copy(unit, index):
        region = x_region(unit, (x, *x_near, x_far)[index], 0, x_rows)
        return remote(region, region, core_send.at[unit, index], core_recv.at[unit, index], twin)

    def x_begin(unit):
        region = x_region(unit, x, 0, x_rows)
        pltpu.make_async_copy(region, region, put_recv.at[unit]).wait()
        for side in range(2):
            x_copy(unit, side).start()
        core_copy(unit, 0).start()

    def x_pass(unit):
        for side in range(2):
            x_copy(unit, side).wait_recv()
        for side in range(2):
            xf_copy(unit, side).start()
        for index in (1, 2):
            core_copy(unit, index).start()

    def x_end(unit):
        for side in range(2):
            xf_copy(unit, side).wait_recv()
        core_copy(unit, 3).start()

    def core_end(unit):
        for index in range(4):
            core_copy(unit, index).wait_recv()

    def forward(step):
        for plan in range(PLANS):
            for side in range(2):
                own_copy(plan, step, side).wait_recv()
            for side in range(2):
                fwd_copy(plan, step, side).start()

    send_own(0, (1, 0))
    send_own(1, *over_y)
    for side in range(2):
        z_copy(side).wait_recv()
    for side in range(2):
        zf_copy(side).start()
    send_own(1, (0, 1), (1, 0))
    send_own(2, (2, 0), (2, 1))
    for side in range(2):
        zf_copy(side).wait_recv()
    for unit in range(PLANS):
        for copy in put_copies(unit, True):
            copy.start()
    send_own(2, (0, 0), (1, 1), (0, 1), (1, 0))
    forward(0)
    for unit in range(PLANS):
        x_begin(unit)
    send_own(3, *over_y, (0, 1), (1, 0))
    forward(1)
    for unit in range(PLANS):
        x_pass(unit)
    for copy in put_copies(OWN, True):
        copy.start()
    forward(2)
    for unit in range(PLANS):
        x_end(unit)
    for unit in range(PLANS):
        core_end(unit)
    forward(3)
    x_begin(OWN)
    local.wait()

    def partner_product(plan, cols):
        rows = slabs[:, :, cols].reshape(4 * height, step_width)
        return jnp.dot(weights[plan], rows, preferred_element_type=F32)

    def own_product(plan, cols):
        result = None
        for slot in range(4):
            apart = (slot % 2) * 2 ** ((plan + 1) % 3) + (slot // 2) * 2 ** ((plan + 2) % 3)
            lanes = pl.ds(apart * height, height)
            term = jnp.dot(own_weights[:, lanes], slabs[slot, :, cols], preferred_element_type=F32)
            result = term if result is None else result + term
        return result

    @pl.loop(0, STEPS)
    def _(step):
        for plan in range(PLANS):
            cols = columns(plan, step)
            for side in range(2):
                fwd_copy(plan, step, side).wait_recv()
            partial[:, cols] = partner_product(plan, cols).astype(BF16)
            sum_copy(plan, step).start()

    for stage in (x_pass, x_end, core_end):
        stage(OWN)

    @pl.loop(0, STEPS)
    def _(step):
        for plan in range(PLANS):
            cols = columns(plan, step)
            total[:, cols] = own_product(plan, cols)

    @pl.loop(0, STEPS)
    def _(step):
        for plan in range(PLANS):
            cols = columns(plan, step)
            sum_copy(plan, step).wait_recv()
            out[:, cols] = (total[:, cols] + arrived[:, cols].astype(F32)).astype(BF16)

    for index in range(3):
        part_copy(index).wait_send()
    for side in range(2):
        z_copy(side).wait_send()
        zf_copy(side).wait_send()
    for unit in range(PLANS + 1):
        for copy in put_copies(unit, False):
            copy.wait_send()
        for side in range(2):
            x_copy(unit, side).wait_send()
            xf_copy(unit, side).wait_send()
        for index in range(4):
            core_copy(unit, index).wait_send()

    @pl.loop(0, STEPS)
    def _(step):
        for plan in range(PLANS):
            for side in range(2):
                own_copy(plan, step, side).wait_send()
                fwd_copy(plan, step, side).wait_send()
            sum_copy(plan, step).wait_send()


def shards(left_rows, right_rows, row_weight, coupling, assign, orders, offsets):
    height, width = left_rows.shape
    band = right_rows.shape[1] * lax.axis_size("tile")
    block = band // lax.axis_size("blk")
    dma = pltpu.SemaphoreType.DMA
    smem = pl.BlockSpec(memory_space=pltpu.SMEM)
    vmem = pl.BlockSpec(memory_space=pltpu.VMEM)
    hbm = pl.BlockSpec(memory_space=pl.ANY)
    return pl.pallas_call(
        kernel,
        out_shape=pltpu.VMEM((block, width), BF16),
        in_specs=[smem, smem, smem, vmem, vmem, vmem, hbm],
        out_specs=vmem,
        scratch_shapes=[
            pltpu.VMEM((4, height, width), BF16),
            pltpu.VMEM((PLANS, block, 4 * height), BF16),
            pltpu.VMEM((block, 8 * height), BF16),
            pltpu.VMEM((right_rows.shape[1], height), BF16),
            pltpu.VMEM((4, 4, right_rows.shape[1] // 4, height), BF16),
            pltpu.VMEM((block, width), BF16),
            pltpu.VMEM((block, width), BF16),
            pltpu.VMEM((block, width), F32),
            dma((PLANS, STEPS, 2)), dma((PLANS, STEPS, 2)),
            dma((PLANS, STEPS, 2)), dma((PLANS, STEPS, 2)),
            dma((PLANS, STEPS)), dma((PLANS, STEPS)),
            dma((2,)), dma((3,)), dma((3,)), dma((2,)), dma((2,)), dma((2,)), dma((2,)),
            dma((PLANS + 1, 7)), dma((PLANS + 1,)),
            dma((PLANS + 1, 2)), dma((PLANS + 1, 2)),
            dma((PLANS + 1, 2)), dma((PLANS + 1, 2)),
            dma((PLANS + 1, 4)), dma((PLANS + 1, 4)),
        ],
        compiler_params=pltpu.CompilerParams(collective_id=0, has_side_effects=True, vmem_limit_bytes=60 * 2**20),
    )(
        assign, orders, offsets, row_weight.reshape(1, height), coupling.reshape(1, height), right_rows, left_rows
    )


def solution(mesh):
    return jax.shard_map(
        shards,
        mesh=mesh,
        in_specs=(P("blk", "tile"), P("blk", "tile"), P("blk"), P("blk"), P(), P(), P()),
        out_specs=P("blk", "tile"),
        check_vma=False,
    )
```

```python
import functools

import jax
import jax.numpy as jnp
from jax import lax
from jax.experimental import pallas as pl
from jax.experimental.pallas import tpu as pltpu
from jax.sharding import PartitionSpec as P

MESH = pl.DeviceIdType.MESH
F32 = jnp.float32
BF16 = jnp.bfloat16
HIGH = lax.Precision.HIGHEST
PLANS = 3
OWN = 3
STEPS = 4


def flip(bit):
    return 1 - bit


def differ(one, other):
    return (one + other) % 2


def ring_bits(place):
    high = place // 2
    return (place + high) % 2, high


def ring_place(low, high):
    return 2 * high + (low + high) % 2


def blk_bits(index):
    low, high = ring_bits(index % 4)
    return low, high, index // 4


def blk_index(bits):
    return bits[2] * 4 + ring_place(bits[0], bits[1])


def weigh(mine, assign, orders, offsets, row_weight, coupling, right):
    n_rows = right.shape[0]
    n_blocks = assign.shape[0]
    slots = lax.broadcasted_iota(jnp.int32, (1, n_rows), 1)
    members, scaled = [], []
    for block in range(n_blocks):
        start = offsets[block]
        inside = (
            (jnp.full((1, n_rows), assign[block], jnp.int32) == mine)
            & (slots >= start)
            & (slots < start + orders[block])
        ).astype(F32)
        members.append(inside)
        scaled.append(inside / jnp.sqrt(jnp.full((1, n_rows), orders[block], jnp.int32).astype(F32)))
    member = jnp.concatenate(members, axis=0)
    shares = jnp.concatenate(scaled, axis=0)
    right_t = right[...].astype(F32).T
    sums = lax.dot_general(
        right_t * coupling[...], member, (((1,), (1,)), ((), ())), precision=HIGH, preferred_element_type=F32
    )
    spread = lax.dot_general(
        sums, shares, (((1,), (0,)), ((), ())), precision=HIGH, preferred_element_type=F32
    )
    live = jnp.sum(member, axis=0, keepdims=True)
    return (live * row_weight[...] * right_t + coupling[...] * spread).astype(BF16)


def kernel(
    assign_in, orders_in, offsets_in, row_weight_in, coupling_in, right_in, left, out,
    assign, orders, offsets, row_weight, coupling, right,
    slabs, weights, own_weights, piece, quarters, partial, arrived, total,
    own_send, own_recv, fwd_send, fwd_recv, sum_send, sum_recv,
    small_sem, local_sem, part_send, part_recv, z_send, z_recv, zf_send, zf_recv, put_send, put_recv,
    x_send, x_recv, xf_send, xf_recv, core_send, core_recv,
):
    height, width = left.shape
    plan_width = width // PLANS
    step_width = plan_width // STEPS
    half = height // 2
    block = weights.shape[1]
    core_rows = block // 2
    x_rows = core_rows // 4
    blk = lax.axis_index("blk")
    tile = lax.axis_index("tile")
    x, z_hi, core = tile // 4, (tile // 2) % 2, tile % 2
    y, z = blk % 4, z_hi * 2 + blk // 4
    bits = blk_bits(blk)
    x_bits, z_bits = ring_bits(x), ring_bits(z)

    def device(x_to, y_to, z_to, core_to):
        return (z_to % 2) * 4 + y_to, x_to * 4 + (z_to // 2) * 2 + core_to

    def across(dim):
        return blk_index([flip(bit) if at == dim else bit for at, bit in enumerate(bits)]), tile

    def moved(place_bits, *flips):
        return ring_place(*[differ(bit, by) for bit, by in zip(place_bits, flips)])

    x_near = [moved(x_bits, 1, 0), moved(x_bits, 0, 1)]
    x_far = moved(x_bits, 1, 1)
    z_near = [moved(z_bits, 1, 0), moved(z_bits, 0, 1)]
    y_bits = bits[:2]
    x_peers = [device(to, y, z, core) for to in (*x_near, x_far)]
    z_peers = [device(x, y, to, core) for to in z_near]
    y_peers = {by: device(x, moved(y_bits, *by), z, core) for by in ((1, 0), (0, 1), (1, 1))}
    twin = device(x, y, z, 1 - core)

    barrier = pltpu.get_barrier_semaphore()
    peers = [*y_peers.values(), *z_peers, *x_peers, twin]
    for peer in peers:
        pl.semaphore_signal(barrier, inc=1, device_id=peer, device_id_type=MESH)
    local = pltpu.make_async_copy(left, slabs.at[0], local_sem.at[0])
    local.start()
    small = ((assign_in, assign), (orders_in, orders), (offsets_in, offsets),
             (row_weight_in, row_weight), (coupling_in, coupling), (right_in, right))
    fetches = [pltpu.make_async_copy(src, dst, small_sem.at[at]) for at, (src, dst) in enumerate(small)]
    for fetch in fetches:
        fetch.start()
    for fetch in fetches:
        fetch.wait()
    piece[...] = weigh(blk, assign, orders, offsets, row_weight, coupling, right)
    pl.semaphore_wait(barrier, len(peers))

    def remote(src, dst, send, recv, peer):
        return pltpu.make_async_remote_copy(
            src_ref=src, dst_ref=dst, send_sem=send, recv_sem=recv,
            device_id=peer, device_id_type=MESH,
        )

    def columns(plan, step):
        return pl.ds(pl.multiple_of(plan * plan_width + step * step_width, step_width), step_width)

    def own_copy(plan, step, side):
        cols = columns(plan, step)
        return remote(
            left.at[:, cols], slabs.at[1 + side, :, cols],
            own_send.at[plan, step, side], own_recv.at[plan, step, side],
            across((plan + 1 + side) % 3),
        )

    def fwd_copy(plan, step, side):
        cols = columns(plan, step)
        rows = pl.ds(side * half, half)
        return remote(
            slabs.at[2 - side, rows, cols], slabs.at[3, rows, cols],
            fwd_send.at[plan, step, side], fwd_recv.at[plan, step, side],
            across((plan + 1 + side) % 3),
        )

    def sum_copy(plan, step):
        cols = columns(plan, step)
        return remote(
            partial.at[:, cols], arrived.at[:, cols],
            sum_send.at[plan, step], sum_recv.at[plan, step], across(plan),
        )

    def send_own(step, *sent):
        for plan, side in sent:
            own_copy(plan, step, side).start()

    over_y = ((0, 0), (1, 1), (2, 0), (2, 1))
    send_own(0, *over_y, (0, 1))


    def quarter(index):
        return piece.at[pl.ds(pl.multiple_of(index * x_rows, x_rows), x_rows), :]

    def part_copy(index):
        place = (*x_near, x_far)[index]
        return remote(
            quarter(place), quarters.at[z, x], part_send.at[index], part_recv.at[index], x_peers[index]
        )

    kept = pltpu.make_async_copy(quarter(x), quarters.at[z, x], local_sem.at[1])
    for index in range(3):
        part_copy(index).start()
    kept.start()

    def z_copy(side):
        return remote(quarters.at[z], quarters.at[z], z_send.at[side], z_recv.at[side], z_peers[side])

    def zf_copy(side):
        part = quarters.at[z_near[1 - side], pl.ds(2 * side, 2)]
        return remote(part, part, zf_send.at[side], zf_recv.at[side], z_peers[side])

    kept.wait()
    for index in range(3):
        part_copy(index).wait_recv()
    for side in range(2):
        z_copy(side).start()

    plane = bits[2]

    def puts(unit):
        if unit == OWN:
            for slot in range(7):
                move = (slot % 2, slot // 2 % 2)
                band = [differ(bits[0], move[0]), differ(bits[1], move[1])]
                yield move, differ(plane, slot // 4), band, plane, slot
            return
        for first in range(2):
            for second in range(2):
                if unit < 2:
                    far, slab_plane = first, second
                    band, move = [None, None], [None, None]
                    band[unit], band[1 - unit] = flip(bits[unit]), differ(bits[1 - unit], far)
                    move[unit], move[1 - unit] = 0, far
                    apart = differ(slab_plane, plane)
                    yield tuple(move), slab_plane, band, plane, apart + 2 * far if unit == 1 else far + 2 * apart
                else:
                    band = [differ(bits[0], first), differ(bits[1], second)]
                    yield (first, second), plane, band, flip(plane), first + 2 * second

    def store(unit):
        return own_weights if unit == OWN else weights.at[unit]

    def x_region(unit, x_from, first, count):
        start = pl.multiple_of(core * core_rows + x_from * x_rows + first, count)
        rows = pl.ds(start, count)
        return own_weights.at[rows, pl.ds(0, 7 * height)] if unit == OWN else weights.at[unit, rows, :]

    def put_copies(unit, with_local):
        for index, (move, slab_plane, band, band_plane, slot) in enumerate(puts(unit)):
            band_z_hi = differ(band[0], band[1])
            band_x = 2 * band_plane + band[1]
            rows = pl.ds(pl.multiple_of(core * core_rows + x * x_rows, x_rows), x_rows)
            lanes = pl.ds(pl.multiple_of(slot * height, height), height)
            src = quarters.at[band_z_hi * 2 + slab_plane, band_x]
            dst = store(unit).at[rows, lanes]
            if move != (0, 0):
                yield remote(src, dst, put_send.at[unit, index], put_recv.at[unit], y_peers[move])
            elif with_local:
                yield pltpu.make_async_copy(src, dst, put_recv.at[unit])

    def x_copy(unit, side):
        region = x_region(unit, x, 0, x_rows)
        return remote(region, region, x_send.at[unit, side], x_recv.at[unit, side], x_peers[side])

    def xf_copy(unit, side):
        region = x_region(unit, x_near[1 - side], side * (x_rows // 2), x_rows // 2)
        return remote(region, region, xf_send.at[unit, side], xf_recv.at[unit, side], x_peers[side])

    def core_copy(unit, index):
        region = x_region(unit, (x, *x_near, x_far)[index], 0, x_rows)
        return remote(region, region, core_send.at[unit, index], core_recv.at[unit, index], twin)

    def x_begin(unit):
        region = x_region(unit, x, 0, x_rows)
        pltpu.make_async_copy(region, region, put_recv.at[unit]).wait()
        for side in range(2):
            x_copy(unit, side).start()
        core_copy(unit, 0).start()

    def x_pass(unit):
        for side in range(2):
            x_copy(unit, side).wait_recv()
        for side in range(2):
            xf_copy(unit, side).start()
        for index in (1, 2):
            core_copy(unit, index).start()

    def x_end(unit):
        for side in range(2):
            xf_copy(unit, side).wait_recv()
        core_copy(unit, 3).start()

    def core_end(unit):
        for index in range(4):
            core_copy(unit, index).wait_recv()

    def forward(step):
        for plan in range(PLANS):
            for side in range(2):
                own_copy(plan, step, side).wait_recv()
            for side in range(2):
                fwd_copy(plan, step, side).start()

    send_own(0, (1, 0))
    send_own(1, *over_y)
    for side in range(2):
        z_copy(side).wait_recv()
    for side in range(2):
        zf_copy(side).start()
    send_own(1, (0, 1), (1, 0))
    send_own(2, (2, 0), (2, 1))
    for side in range(2):
        zf_copy(side).wait_recv()
    for unit in range(PLANS):
        for copy in put_copies(unit, True):
            copy.start()
    send_own(2, (0, 0), (1, 1), (0, 1), (1, 0))
    forward(0)
    for unit in range(PLANS):
        x_begin(unit)
    send_own(3, *over_y, (0, 1), (1, 0))
    forward(1)
    for unit in range(PLANS):
        x_pass(unit)
    for copy in put_copies(OWN, True):
        copy.start()
    forward(2)
    for unit in range(PLANS):
        x_end(unit)
    for unit in range(PLANS):
        core_end(unit)
    forward(3)
    x_begin(OWN)
    local.wait()

    def partner_product(plan, cols):
        rows = slabs[:, :, cols].reshape(4 * height, step_width)
        return jnp.dot(weights[plan], rows, preferred_element_type=F32)

    def own_product(plan, cols):
        result = None
        for slot in range(4):
            apart = (slot % 2) * 2 ** ((plan + 1) % 3) + (slot // 2) * 2 ** ((plan + 2) % 3)
            lanes = pl.ds(apart * height, height)
            term = jnp.dot(own_weights[:, lanes], slabs[slot, :, cols], preferred_element_type=F32)
            result = term if result is None else result + term
        return result

    @pl.loop(0, STEPS)
    def _(step):
        for plan in range(PLANS):
            cols = columns(plan, step)
            for side in range(2):
                fwd_copy(plan, step, side).wait_recv()
            partial[:, cols] = partner_product(plan, cols).astype(BF16)
            sum_copy(plan, step).start()

    for stage in (x_pass, x_end, core_end):
        stage(OWN)

    @pl.loop(0, STEPS)
    def _(step):
        for plan in range(PLANS):
            cols = columns(plan, step)
            total[:, cols] = own_product(plan, cols)

    for index in range(3):
        part_copy(index).wait_send()
    for side in range(2):
        z_copy(side).wait_send()
        zf_copy(side).wait_send()
    for unit in range(PLANS + 1):
        for copy in put_copies(unit, False):
            copy.wait_send()
        for side in range(2):
            x_copy(unit, side).wait_send()
            xf_copy(unit, side).wait_send()
        for index in range(4):
            core_copy(unit, index).wait_send()

    @pl.loop(0, STEPS)
    def _(step):
        for plan in range(PLANS):
            for side in range(2):
                own_copy(plan, step, side).wait_send()
                fwd_copy(plan, step, side).wait_send()

    @pl.loop(0, STEPS)
    def _(step):
        for plan in range(PLANS):
            cols = columns(plan, step)
            sum_copy(plan, step).wait_recv()
            out[:, cols] = (total[:, cols] + arrived[:, cols].astype(F32)).astype(BF16)
            sum_copy(plan, step).wait_send()


def shards(left_rows, right_rows, row_weight, coupling, assign, orders, offsets):
    height, width = left_rows.shape
    band = right_rows.shape[1] * lax.axis_size("tile")
    block = band // lax.axis_size("blk")
    dma = pltpu.SemaphoreType.DMA
    vmem = pl.BlockSpec(memory_space=pltpu.VMEM)
    hbm = pl.BlockSpec(memory_space=pl.ANY)
    return pl.pallas_call(
        kernel,
        out_shape=pltpu.VMEM((block, width), BF16),
        in_specs=[hbm] * 7,
        out_specs=vmem,
        scratch_shapes=[
            *[pltpu.SMEM(assign.shape, jnp.int32)] * 3,
            pltpu.VMEM((1, height), F32), pltpu.VMEM((1, height), F32), pltpu.VMEM(right_rows.shape, BF16),
            pltpu.VMEM((4, height, width), BF16),
            pltpu.VMEM((PLANS, block, 4 * height), BF16),
            pltpu.VMEM((block, 8 * height), BF16),
            pltpu.VMEM((right_rows.shape[1], height), BF16),
            pltpu.VMEM((4, 4, right_rows.shape[1] // 4, height), BF16),
            pltpu.VMEM((block, width), BF16),
            pltpu.VMEM((block, width), BF16),
            pltpu.VMEM((block, width), F32),
            dma((PLANS, STEPS, 2)), dma((PLANS, STEPS, 2)),
            dma((PLANS, STEPS, 2)), dma((PLANS, STEPS, 2)),
            dma((PLANS, STEPS)), dma((PLANS, STEPS)),
            dma((6,)), dma((2,)), dma((3,)), dma((3,)), dma((2,)), dma((2,)), dma((2,)), dma((2,)),
            dma((PLANS + 1, 7)), dma((PLANS + 1,)),
            dma((PLANS + 1, 2)), dma((PLANS + 1, 2)),
            dma((PLANS + 1, 2)), dma((PLANS + 1, 2)),
            dma((PLANS + 1, 4)), dma((PLANS + 1, 4)),
        ],
        compiler_params=pltpu.CompilerParams(collective_id=0, has_side_effects=True, vmem_limit_bytes=60 * 2**20),
    )(
        assign, orders, offsets, row_weight.reshape(1, height), coupling.reshape(1, height), right_rows, left_rows
    )


def solution(mesh):
    return jax.shard_map(
        shards,
        mesh=mesh,
        in_specs=(P("blk", "tile"), P("blk", "tile"), P("blk"), P("blk"), P(), P(), P()),
        out_specs=P("blk", "tile"),
        check_vma=False,
    )
```

```python
import functools

import jax
import jax.numpy as jnp
from jax import lax
from jax.experimental import pallas as pl
from jax.experimental.pallas import tpu as pltpu
from jax.sharding import PartitionSpec as P

MESH = pl.DeviceIdType.MESH
F32 = jnp.float32
BF16 = jnp.bfloat16
HIGH = lax.Precision.HIGHEST
PLANS = 3
OWN = 3
FORWARD_ROWS = ((112, 144), (144, 112), (128, 128))
STEPS = 4


def flip(bit):
    return 1 - bit


def differ(one, other):
    return (one + other) % 2


def ring_bits(place):
    high = place // 2
    return (place + high) % 2, high


def ring_place(low, high):
    return 2 * high + (low + high) % 2


def blk_bits(index):
    low, high = ring_bits(index % 4)
    return low, high, index // 4


def blk_index(bits):
    return bits[2] * 4 + ring_place(bits[0], bits[1])


def weigh(mine, assign, orders, offsets, row_weight, coupling, right):
    n_rows = right.shape[0]
    n_blocks = assign.shape[0]
    slots = lax.broadcasted_iota(jnp.int32, (1, n_rows), 1)
    members, scaled = [], []
    for block in range(n_blocks):
        start = offsets[block]
        inside = (
            (jnp.full((1, n_rows), assign[block], jnp.int32) == mine)
            & (slots >= start)
            & (slots < start + orders[block])
        ).astype(F32)
        members.append(inside)
        scaled.append(inside / jnp.sqrt(jnp.full((1, n_rows), orders[block], jnp.int32).astype(F32)))
    member = jnp.concatenate(members, axis=0)
    shares = jnp.concatenate(scaled, axis=0)
    right_t = right[...].astype(F32).T
    sums = lax.dot_general(
        right_t * coupling[...], member, (((1,), (1,)), ((), ())), precision=HIGH, preferred_element_type=F32
    )
    spread = lax.dot_general(
        sums, shares, (((1,), (0,)), ((), ())), precision=HIGH, preferred_element_type=F32
    )
    live = jnp.sum(member, axis=0, keepdims=True)
    return (live * row_weight[...] * right_t + coupling[...] * spread).astype(BF16)


def kernel(
    assign_in, orders_in, offsets_in, row_weight_in, coupling_in, right_in, left, out,
    assign, orders, offsets, row_weight, coupling, right,
    slabs, weights, own_weights, piece, quarters, partial, arrived, total,
    own_send, own_recv, fwd_send, fwd_recv, sum_send, sum_recv,
    small_sem, local_sem, part_send, part_recv, z_send, z_recv, zf_send, zf_recv, put_send, put_recv,
    x_send, x_recv, xf_send, xf_recv, core_send, core_recv,
):
    height, width = left.shape
    plan_width = width // PLANS
    step_width = plan_width // STEPS
    block = weights.shape[1]
    core_rows = block // 2
    x_rows = core_rows // 4
    blk = lax.axis_index("blk")
    tile = lax.axis_index("tile")
    x, z_hi, core = tile // 4, (tile // 2) % 2, tile % 2
    y, z = blk % 4, z_hi * 2 + blk // 4
    bits = blk_bits(blk)
    x_bits, z_bits = ring_bits(x), ring_bits(z)

    def device(x_to, y_to, z_to, core_to):
        return (z_to % 2) * 4 + y_to, x_to * 4 + (z_to // 2) * 2 + core_to

    def across(dim):
        return blk_index([flip(bit) if at == dim else bit for at, bit in enumerate(bits)]), tile

    def moved(place_bits, *flips):
        return ring_place(*[differ(bit, by) for bit, by in zip(place_bits, flips)])

    x_near = [moved(x_bits, 1, 0), moved(x_bits, 0, 1)]
    x_far = moved(x_bits, 1, 1)
    z_near = [moved(z_bits, 1, 0), moved(z_bits, 0, 1)]
    y_bits = bits[:2]
    x_peers = [device(to, y, z, core) for to in (*x_near, x_far)]
    z_peers = [device(x, y, to, core) for to in z_near]
    y_peers = {by: device(x, moved(y_bits, *by), z, core) for by in ((1, 0), (0, 1), (1, 1))}
    twin = device(x, y, z, 1 - core)

    barrier = pltpu.get_barrier_semaphore()
    peers = [*y_peers.values(), *z_peers, *x_peers, twin]
    for peer in peers:
        pl.semaphore_signal(barrier, inc=1, device_id=peer, device_id_type=MESH)
    local = pltpu.make_async_copy(left, slabs.at[0], local_sem.at[0])
    local.start()
    small = ((assign_in, assign), (orders_in, orders), (offsets_in, offsets),
             (row_weight_in, row_weight), (coupling_in, coupling), (right_in, right))
    fetches = [pltpu.make_async_copy(src, dst, small_sem.at[at]) for at, (src, dst) in enumerate(small)]
    for fetch in fetches:
        fetch.start()
    for fetch in fetches:
        fetch.wait()
    piece[...] = weigh(blk, assign, orders, offsets, row_weight, coupling, right)
    pl.semaphore_wait(barrier, len(peers))

    def remote(src, dst, send, recv, peer):
        return pltpu.make_async_remote_copy(
            src_ref=src, dst_ref=dst, send_sem=send, recv_sem=recv,
            device_id=peer, device_id_type=MESH,
        )

    def columns(plan, step):
        return pl.ds(pl.multiple_of(plan * plan_width + step * step_width, step_width), step_width)

    def own_copy(plan, step, side):
        cols = columns(plan, step)
        return remote(
            left.at[:, cols], slabs.at[1 + side, :, cols],
            own_send.at[plan, step, side], own_recv.at[plan, step, side],
            across((plan + 1 + side) % 3),
        )

    def fwd_copy(plan, step, side):
        cols = columns(plan, step)
        shares = FORWARD_ROWS[plan]
        rows = pl.ds(side * shares[0], shares[side])
        return remote(
            slabs.at[2 - side, rows, cols], slabs.at[3, rows, cols],
            fwd_send.at[plan, step, side], fwd_recv.at[plan, step, side],
            across((plan + 1 + side) % 3),
        )

    def sum_copy(plan, step, part):
        cols = columns(plan, step)
        rows = pl.ds(part * core_rows, core_rows)
        return remote(
            partial.at[rows, cols], arrived.at[rows, cols],
            sum_send.at[plan, step, part], sum_recv.at[plan, step, part], across(plan),
        )

    def send_own(step, *sent):
        for plan, side in sent:
            own_copy(plan, step, side).start()

    over_y = ((0, 0), (1, 1), (2, 0), (2, 1))
    send_own(0, *over_y, (0, 1))


    def quarter(index):
        return piece.at[pl.ds(pl.multiple_of(index * x_rows, x_rows), x_rows), :]

    def part_copy(index):
        place = (*x_near, x_far)[index]
        return remote(
            quarter(place), quarters.at[z, x], part_send.at[index], part_recv.at[index], x_peers[index]
        )

    kept = pltpu.make_async_copy(quarter(x), quarters.at[z, x], local_sem.at[1])
    for index in range(3):
        part_copy(index).start()
    kept.start()

    plane = bits[2]

    def z_copies(side):
        for at, part in enumerate((pl.ds(2 * flip(plane), 2), pl.ds(2 * plane + side, 1))):
            region = quarters.at[z, part]
            yield remote(region, region, z_send.at[side, at], z_recv.at[side, at], z_peers[side])

    def zf_copies(side):
        for at, place in enumerate((plane, flip(plane))):
            region = quarters.at[z_near[1 - side], 2 * place + 1 - side]
            yield remote(region, region, zf_send.at[side, at], zf_recv.at[side, at], z_peers[side])

    def each(copies, act):
        for side in range(2):
            for copy in copies(side):
                getattr(copy, act)()

    kept.wait()
    for index in range(3):
        part_copy(index).wait_recv()
    each(z_copies, "start")

    def puts(unit):
        if unit == OWN:
            for slot in range(7):
                move = (slot % 2, slot // 2 % 2)
                band = [differ(bits[0], move[0]), differ(bits[1], move[1])]
                yield move, differ(plane, slot // 4), band, plane, slot
            return
        for first in range(2):
            for second in range(2):
                if unit < 2:
                    far, slab_plane = first, second
                    band, move = [None, None], [None, None]
                    band[unit], band[1 - unit] = flip(bits[unit]), differ(bits[1 - unit], far)
                    move[unit], move[1 - unit] = 0, far
                    apart = differ(slab_plane, plane)
                    yield tuple(move), slab_plane, band, plane, apart + 2 * far if unit == 1 else far + 2 * apart
                else:
                    band = [differ(bits[0], first), differ(bits[1], second)]
                    yield (first, second), plane, band, flip(plane), first + 2 * second

    def store(unit):
        return own_weights if unit == OWN else weights.at[unit]

    def x_region(unit, x_from, first, count):
        start = pl.multiple_of(core * core_rows + x_from * x_rows + first, count)
        rows = pl.ds(start, count)
        return own_weights.at[rows, pl.ds(0, 7 * height)] if unit == OWN else weights.at[unit, rows, :]

    def put_copies(unit, with_local):
        for index, (move, slab_plane, band, band_plane, slot) in enumerate(puts(unit)):
            band_z_hi = differ(band[0], band[1])
            band_x = 2 * band_plane + band[1]
            rows = pl.ds(pl.multiple_of(core * core_rows + x * x_rows, x_rows), x_rows)
            lanes = pl.ds(pl.multiple_of(slot * height, height), height)
            src = quarters.at[band_z_hi * 2 + slab_plane, band_x]
            dst = store(unit).at[rows, lanes]
            if move != (0, 0):
                yield remote(src, dst, put_send.at[unit, index], put_recv.at[unit], y_peers[move])
            elif with_local:
                yield pltpu.make_async_copy(src, dst, put_recv.at[unit])

    def x_copy(unit, side):
        region = x_region(unit, x, 0, x_rows)
        return remote(region, region, x_send.at[unit, side], x_recv.at[unit, side], x_peers[side])

    def xf_copy(unit, side):
        region = x_region(unit, x_near[1 - side], side * (x_rows // 2), x_rows // 2)
        return remote(region, region, xf_send.at[unit, side], xf_recv.at[unit, side], x_peers[side])

    def core_copy(unit, index):
        region = x_region(unit, (x, *x_near, x_far)[index], 0, x_rows)
        return remote(region, region, core_send.at[unit, index], core_recv.at[unit, index], twin)

    def x_begin(unit):
        region = x_region(unit, x, 0, x_rows)
        pltpu.make_async_copy(region, region, put_recv.at[unit]).wait()
        for side in range(2):
            x_copy(unit, side).start()
        core_copy(unit, 0).start()

    def x_pass(unit):
        for side in range(2):
            x_copy(unit, side).wait_recv()
        for side in range(2):
            xf_copy(unit, side).start()
        for index in (1, 2):
            core_copy(unit, index).start()

    def x_end(unit):
        for side in range(2):
            xf_copy(unit, side).wait_recv()
        core_copy(unit, 3).start()

    def core_end(unit):
        for index in range(4):
            core_copy(unit, index).wait_recv()

    def forward(step):
        for plan in range(PLANS):
            for side in range(2):
                own_copy(plan, step, side).wait_recv()
            for side in range(2):
                fwd_copy(plan, step, side).start()

    send_own(0, (1, 0))
    send_own(1, *over_y)
    each(z_copies, "wait_recv")
    each(zf_copies, "start")
    send_own(1, (0, 1), (1, 0))
    send_own(2, (2, 0), (2, 1))
    each(zf_copies, "wait_recv")
    for unit in range(PLANS):
        for copy in put_copies(unit, True):
            copy.start()
    send_own(2, (0, 0), (1, 1), (0, 1), (1, 0))
    forward(0)
    for unit in range(PLANS):
        x_begin(unit)
    send_own(3, *over_y, (0, 1), (1, 0))
    forward(1)
    for unit in range(PLANS):
        x_pass(unit)
    forward(2)
    for copy in put_copies(OWN, True):
        copy.start()
    for unit in range(PLANS):
        x_end(unit)
    forward(3)
    for unit in range(PLANS):
        core_end(unit)
    x_begin(OWN)
    local.wait()

    def partner_product(plan, cols):
        rows = slabs[:, :, cols].reshape(4 * height, step_width)
        return jnp.dot(weights[plan], rows, preferred_element_type=F32)

    def own_product(plan, cols):
        result = None
        for slot in range(4):
            apart = (slot % 2) * 2 ** ((plan + 1) % 3) + (slot // 2) * 2 ** ((plan + 2) % 3)
            lanes = pl.ds(apart * height, height)
            term = jnp.dot(own_weights[:, lanes], slabs[slot, :, cols], preferred_element_type=F32)
            result = term if result is None else result + term
        return result

    @pl.loop(0, STEPS)
    def _(step):
        for plan in range(PLANS):
            cols = columns(plan, step)
            for side in range(2):
                fwd_copy(plan, step, side).wait_recv()
            partial[:, cols] = partner_product(plan, cols).astype(BF16)
            for part in range(2):
                sum_copy(plan, step, part).start()

    for stage in (x_pass, x_end, core_end):
        stage(OWN)

    @pl.loop(0, STEPS)
    def _(step):
        for plan in range(PLANS):
            cols = columns(plan, step)
            total[:, cols] = own_product(plan, cols)

    for index in range(3):
        part_copy(index).wait_send()
    each(z_copies, "wait_send")
    each(zf_copies, "wait_send")
    for unit in range(PLANS + 1):
        for copy in put_copies(unit, False):
            copy.wait_send()
        for side in range(2):
            x_copy(unit, side).wait_send()
            xf_copy(unit, side).wait_send()
        for index in range(4):
            core_copy(unit, index).wait_send()

    @pl.loop(0, STEPS)
    def _(step):
        for plan in range(PLANS):
            for side in range(2):
                own_copy(plan, step, side).wait_send()
                fwd_copy(plan, step, side).wait_send()

    @pl.loop(0, STEPS)
    def _(step):
        for part in range(2):
            rows = pl.ds(part * core_rows, core_rows)
            for plan in range(PLANS):
                cols = columns(plan, step)
                sum_copy(plan, step, part).wait()
                out[rows, cols] = (total[rows, cols] + arrived[rows, cols].astype(F32)).astype(BF16)


def shards(left_rows, right_rows, row_weight, coupling, assign, orders, offsets):
    height, width = left_rows.shape
    band = right_rows.shape[1] * lax.axis_size("tile")
    block = band // lax.axis_size("blk")
    dma = pltpu.SemaphoreType.DMA
    vmem = pl.BlockSpec(memory_space=pltpu.VMEM)
    hbm = pl.BlockSpec(memory_space=pl.ANY)
    return pl.pallas_call(
        kernel,
        out_shape=pltpu.VMEM((block, width), BF16),
        in_specs=[hbm] * 7,
        out_specs=vmem,
        scratch_shapes=[
            *[pltpu.SMEM(assign.shape, jnp.int32)] * 3,
            pltpu.VMEM((1, height), F32), pltpu.VMEM((1, height), F32), pltpu.VMEM(right_rows.shape, BF16),
            pltpu.VMEM((4, height, width), BF16),
            pltpu.VMEM((PLANS, block, 4 * height), BF16),
            pltpu.VMEM((block, 8 * height), BF16),
            pltpu.VMEM((right_rows.shape[1], height), BF16),
            pltpu.VMEM((4, 4, right_rows.shape[1] // 4, height), BF16),
            pltpu.VMEM((block, width), BF16),
            pltpu.VMEM((block, width), BF16),
            pltpu.VMEM((block, width), F32),
            dma((PLANS, STEPS, 2)), dma((PLANS, STEPS, 2)),
            dma((PLANS, STEPS, 2)), dma((PLANS, STEPS, 2)),
            dma((PLANS, STEPS, 2)), dma((PLANS, STEPS, 2)),
            dma((6,)), dma((2,)), dma((3,)), dma((3,)), dma((2, 2)), dma((2, 2)), dma((2, 2)), dma((2, 2)),
            dma((PLANS + 1, 7)), dma((PLANS + 1,)),
            dma((PLANS + 1, 2)), dma((PLANS + 1, 2)),
            dma((PLANS + 1, 2)), dma((PLANS + 1, 2)),
            dma((PLANS + 1, 4)), dma((PLANS + 1, 4)),
        ],
        compiler_params=pltpu.CompilerParams(collective_id=0, has_side_effects=True, vmem_limit_bytes=60 * 2**20),
    )(
        assign, orders, offsets, row_weight.reshape(1, height), coupling.reshape(1, height), right_rows, left_rows
    )


def solution(mesh):
    return jax.shard_map(
        shards,
        mesh=mesh,
        in_specs=(P("blk", "tile"), P("blk", "tile"), P("blk"), P("blk"), P(), P(), P()),
        out_specs=P("blk", "tile"),
        check_vma=False,
    )
```

```python
import functools

import jax
import jax.numpy as jnp
from jax import lax
from jax.experimental import pallas as pl
from jax.experimental.pallas import tpu as pltpu
from jax.sharding import PartitionSpec as P

MESH = pl.DeviceIdType.MESH
F32 = jnp.float32
BF16 = jnp.bfloat16
HIGH = lax.Precision.HIGHEST
PLANS = 3
OWN = 3
SHIFTED = 3
FORWARD_ROWS = ((112, 144), (144, 112), (128, 128))
STEPS = 4


def flip(bit):
    return 1 - bit


def differ(one, other):
    return (one + other) % 2


def ring_bits(place):
    high = place // 2
    return (place + high) % 2, high


def ring_place(low, high):
    return 2 * high + (low + high) % 2


def blk_bits(index):
    low, high = ring_bits(index % 4)
    return low, high, index // 4


def blk_index(bits):
    return bits[2] * 4 + ring_place(bits[0], bits[1])


def weigh(mine, assign, orders, offsets, row_weight, coupling, right):
    n_rows = right.shape[0]
    n_blocks = assign.shape[0]
    slots = lax.broadcasted_iota(jnp.int32, (1, n_rows), 1)
    members, scaled = [], []
    for block in range(n_blocks):
        start = offsets[block]
        inside = (
            (jnp.full((1, n_rows), assign[block], jnp.int32) == mine)
            & (slots >= start)
            & (slots < start + orders[block])
        ).astype(F32)
        members.append(inside)
        scaled.append(inside / jnp.sqrt(jnp.full((1, n_rows), orders[block], jnp.int32).astype(F32)))
    member = jnp.concatenate(members, axis=0)
    shares = jnp.concatenate(scaled, axis=0)
    right_t = right[...].astype(F32).T
    sums = lax.dot_general(
        right_t * coupling[...], member, (((1,), (1,)), ((), ())), precision=HIGH, preferred_element_type=F32
    )
    spread = lax.dot_general(
        sums, shares, (((1,), (0,)), ((), ())), precision=HIGH, preferred_element_type=F32
    )
    live = jnp.sum(member, axis=0, keepdims=True)
    return (live * row_weight[...] * right_t + coupling[...] * spread).astype(BF16)


def kernel(
    assign_in, orders_in, offsets_in, row_weight_in, coupling_in, right_in, left, out,
    assign, orders, offsets, row_weight, coupling, right,
    slabs, weights, own_weights, piece, quarters, partial, arrived, total,
    own_send, own_recv, fwd_send, fwd_recv, sum_send, sum_recv,
    small_sem, local_sem, part_send, part_recv, z_send, z_recv, zf_send, zf_recv, put_send, put_recv, chain_send,
    x_send, x_recv, xf_send, xf_recv, core_send, core_recv,
):
    height, width = left.shape
    plan_width = width // PLANS
    step_width = plan_width // STEPS
    block = weights.shape[1]
    core_rows = block // 2
    x_rows = core_rows // 4
    blk = lax.axis_index("blk")
    tile = lax.axis_index("tile")
    x, z_hi, core = tile // 4, (tile // 2) % 2, tile % 2
    y, z = blk % 4, z_hi * 2 + blk // 4
    bits = blk_bits(blk)
    x_bits, z_bits = ring_bits(x), ring_bits(z)

    def device(x_to, y_to, z_to, core_to):
        return (z_to % 2) * 4 + y_to, x_to * 4 + (z_to // 2) * 2 + core_to

    def across(dim):
        return blk_index([flip(bit) if at == dim else bit for at, bit in enumerate(bits)]), tile

    def moved(place_bits, *flips):
        return ring_place(*[differ(bit, by) for bit, by in zip(place_bits, flips)])

    x_near = [moved(x_bits, 1, 0), moved(x_bits, 0, 1)]
    x_far = moved(x_bits, 1, 1)
    z_near = [moved(z_bits, 1, 0), moved(z_bits, 0, 1)]
    y_bits = bits[:2]
    x_peers = [device(to, y, z, core) for to in (*x_near, x_far)]
    z_peers = [device(x, y, to, core) for to in z_near]
    y_peers = {by: device(x, moved(y_bits, *by), z, core) for by in ((1, 0), (0, 1), (1, 1))}
    twin = device(x, y, z, 1 - core)

    barrier = pltpu.get_barrier_semaphore()
    peers = [*y_peers.values(), *z_peers, *x_peers, twin]
    for peer in peers:
        pl.semaphore_signal(barrier, inc=1, device_id=peer, device_id_type=MESH)
    local = pltpu.make_async_copy(left, slabs.at[0], local_sem.at[0])
    local.start()
    small = ((assign_in, assign), (orders_in, orders), (offsets_in, offsets),
             (row_weight_in, row_weight), (coupling_in, coupling), (right_in, right))
    fetches = [pltpu.make_async_copy(src, dst, small_sem.at[at]) for at, (src, dst) in enumerate(small)]
    for fetch in fetches:
        fetch.start()
    for fetch in fetches:
        fetch.wait()
    piece[...] = weigh(blk, assign, orders, offsets, row_weight, coupling, right)
    pl.semaphore_wait(barrier, len(peers))

    def remote(src, dst, send, recv, peer):
        return pltpu.make_async_remote_copy(
            src_ref=src, dst_ref=dst, send_sem=send, recv_sem=recv,
            device_id=peer, device_id_type=MESH,
        )

    def columns(plan, step):
        return pl.ds(pl.multiple_of(plan * plan_width + step * step_width, step_width), step_width)

    def own_copy(plan, step, side):
        cols = columns(plan, step)
        return remote(
            left.at[:, cols], slabs.at[1 + side, :, cols],
            own_send.at[plan, step, side], own_recv.at[plan, step, side],
            across((plan + 1 + side) % 3),
        )

    def fwd_copy(plan, step, side):
        cols = columns(plan, step)
        shares = FORWARD_ROWS[plan] if step < SHIFTED else (128, 128)
        rows = pl.ds(side * shares[0], shares[side])
        return remote(
            slabs.at[2 - side, rows, cols], slabs.at[3, rows, cols],
            fwd_send.at[plan, step, side], fwd_recv.at[plan, step, side],
            across((plan + 1 + side) % 3),
        )

    def sum_copy(plan, step, part):
        cols = columns(plan, step)
        rows = pl.ds(part * core_rows, core_rows)
        return remote(
            partial.at[rows, cols], arrived.at[rows, cols],
            sum_send.at[plan, step, part], sum_recv.at[plan, step, part], across(plan),
        )

    def send_own(step, *sent):
        for plan, side in sent:
            own_copy(plan, step, side).start()

    over_y = ((0, 0), (1, 1), (2, 0), (2, 1))
    send_own(0, *over_y, (0, 1))


    def quarter(index):
        return piece.at[pl.ds(pl.multiple_of(index * x_rows, x_rows), x_rows), :]

    def part_copy(index):
        place = (*x_near, x_far)[index]
        return remote(
            quarter(place), quarters.at[z, x], part_send.at[index], part_recv.at[index], x_peers[index]
        )

    kept = pltpu.make_async_copy(quarter(x), quarters.at[z, x], local_sem.at[1])
    for index in range(3):
        part_copy(index).start()
    kept.start()

    plane = bits[2]

    def z_copies(side):
        for at, part in enumerate((pl.ds(2 * flip(plane), 2), pl.ds(2 * plane + side, 1))):
            region = quarters.at[z, part]
            yield remote(region, region, z_send.at[side, at], z_recv.at[side, at], z_peers[side])

    def zf_copies(side):
        for at, place in enumerate((plane, flip(plane))):
            region = quarters.at[z_near[1 - side], 2 * place + 1 - side]
            yield remote(region, region, zf_send.at[side, at], zf_recv.at[side, at], z_peers[side])

    def each(copies, act):
        for side in range(2):
            for copy in copies(side):
                getattr(copy, act)()

    kept.wait()
    for index in range(3):
        part_copy(index).wait_recv()
    each(z_copies, "start")

    def puts(unit):
        if unit == OWN:
            for slot in (0, 1, 2, 4, 5, 6):
                move = (slot % 2, slot // 2 % 2)
                band = [differ(bits[0], move[0]), differ(bits[1], move[1])]
                yield move, differ(plane, slot // 4), band, plane, slot
            return
        for first in range(2):
            for second in range(2):
                if unit < 2:
                    far, slab_plane = first, second
                    band, move = [None, None], [None, None]
                    band[unit], band[1 - unit] = flip(bits[unit]), differ(bits[1 - unit], far)
                    move[unit], move[1 - unit] = 0, far
                    apart = differ(slab_plane, plane)
                    yield tuple(move), slab_plane, band, plane, apart + 2 * far if unit == 1 else far + 2 * apart
                else:
                    band = [differ(bits[0], first), differ(bits[1], second)]
                    yield (first, second), plane, band, flip(plane), first + 2 * second

    def store(unit):
        return own_weights if unit == OWN else weights.at[unit]

    def x_region(unit, x_from, first, count):
        start = pl.multiple_of(core * core_rows + x_from * x_rows + first, count)
        rows = pl.ds(start, count)
        return own_weights.at[rows, pl.ds(0, 7 * height)] if unit == OWN else weights.at[unit, rows, :]

    def put_copies(unit, with_local):
        for index, (move, slab_plane, band, band_plane, slot) in enumerate(puts(unit)):
            band_z_hi = differ(band[0], band[1])
            band_x = 2 * band_plane + band[1]
            rows = pl.ds(pl.multiple_of(core * core_rows + x * x_rows, x_rows), x_rows)
            lanes = pl.ds(pl.multiple_of(slot * height, height), height)
            src = quarters.at[band_z_hi * 2 + slab_plane, band_x]
            dst = store(unit).at[rows, lanes]
            if move != (0, 0):
                yield remote(src, dst, put_send.at[unit, index], put_recv.at[unit], y_peers[move])
            elif with_local:
                yield pltpu.make_async_copy(src, dst, put_recv.at[unit])

    def chain_copy(side):
        count = x_rows // 2
        start = pl.multiple_of(core * core_rows + x * x_rows + side * count, count)
        rows = pl.ds(start, count)
        return remote(
            weights.at[1 - side, rows, pl.ds((2 - side) * height, height)],
            own_weights.at[rows, pl.ds(3 * height, height)],
            chain_send.at[side], put_recv.at[OWN], y_peers[(side, 1 - side)],
        )

    def x_copy(unit, side):
        region = x_region(unit, x, 0, x_rows)
        return remote(region, region, x_send.at[unit, side], x_recv.at[unit, side], x_peers[side])

    def xf_copy(unit, side):
        region = x_region(unit, x_near[1 - side], side * (x_rows // 2), x_rows // 2)
        return remote(region, region, xf_send.at[unit, side], xf_recv.at[unit, side], x_peers[side])

    def core_copy(unit, index):
        region = x_region(unit, (x, *x_near, x_far)[index], 0, x_rows)
        return remote(region, region, core_send.at[unit, index], core_recv.at[unit, index], twin)

    def x_begin(unit):
        region = x_region(unit, x, 0, x_rows)
        pltpu.make_async_copy(region, region, put_recv.at[unit]).wait()
        for side in range(2):
            x_copy(unit, side).start()
        core_copy(unit, 0).start()

    def x_pass(unit):
        for side in range(2):
            x_copy(unit, side).wait_recv()
        for side in range(2):
            xf_copy(unit, side).start()
        for index in (1, 2):
            core_copy(unit, index).start()

    def x_end(unit):
        for side in range(2):
            xf_copy(unit, side).wait_recv()
        core_copy(unit, 3).start()

    def core_end(unit):
        for index in range(4):
            core_copy(unit, index).wait_recv()

    def forward(step):
        for plan in range(PLANS):
            for side in range(2):
                own_copy(plan, step, side).wait_recv()
            for side in range(2):
                fwd_copy(plan, step, side).start()

    send_own(0, (1, 0))
    send_own(1, *over_y)
    each(z_copies, "wait_recv")
    each(zf_copies, "start")
    send_own(1, (0, 1), (1, 0))
    send_own(2, (2, 0), (2, 1))
    each(zf_copies, "wait_recv")
    for unit in range(PLANS):
        for copy in put_copies(unit, True):
            copy.start()
    send_own(2, (0, 0), (1, 1), (0, 1), (1, 0))
    forward(0)
    for unit in range(PLANS):
        x_begin(unit)
    send_own(3, *over_y, (0, 1), (1, 0))
    forward(1)
    for unit in range(PLANS):
        x_pass(unit)
    forward(2)
    for copy in put_copies(OWN, True):
        copy.start()
    for side in range(2):
        chain_copy(side).start()
    for unit in range(PLANS):
        x_end(unit)
    forward(3)
    for unit in range(PLANS):
        core_end(unit)
    x_begin(OWN)
    local.wait()

    def partner_product(plan, cols):
        rows = slabs[:, :, cols].reshape(4 * height, step_width)
        return jnp.dot(weights[plan], rows, preferred_element_type=F32)

    def own_product(plan, cols):
        result = None
        for slot in range(4):
            apart = (slot % 2) * 2 ** ((plan + 1) % 3) + (slot // 2) * 2 ** ((plan + 2) % 3)
            lanes = pl.ds(apart * height, height)
            term = jnp.dot(own_weights[:, lanes], slabs[slot, :, cols], preferred_element_type=F32)
            result = term if result is None else result + term
        return result

    for step in range(STEPS):
        for plan in range(PLANS):
            cols = columns(plan, step)
            for side in range(2):
                fwd_copy(plan, step, side).wait_recv()
            partial[:, cols] = partner_product(plan, cols).astype(BF16)
            for part in range(2):
                sum_copy(plan, step, part).start()

    for stage in (x_pass, x_end, core_end):
        stage(OWN)

    @pl.loop(0, STEPS)
    def _(step):
        for plan in range(PLANS):
            cols = columns(plan, step)
            total[:, cols] = own_product(plan, cols)

    for index in range(3):
        part_copy(index).wait_send()
    each(z_copies, "wait_send")
    for side in range(2):
        chain_copy(side).wait_send()
    each(zf_copies, "wait_send")
    for unit in range(PLANS + 1):
        for copy in put_copies(unit, False):
            copy.wait_send()
        for side in range(2):
            x_copy(unit, side).wait_send()
            xf_copy(unit, side).wait_send()
        for index in range(4):
            core_copy(unit, index).wait_send()

    for step in range(STEPS):
        for plan in range(PLANS):
            for side in range(2):
                own_copy(plan, step, side).wait_send()
                fwd_copy(plan, step, side).wait_send()

    @pl.loop(0, STEPS)
    def _(step):
        for part in range(2):
            rows = pl.ds(part * core_rows, core_rows)
            for plan in range(PLANS):
                cols = columns(plan, step)
                sum_copy(plan, step, part).wait()
                out[rows, cols] = (total[rows, cols] + arrived[rows, cols].astype(F32)).astype(BF16)


def shards(left_rows, right_rows, row_weight, coupling, assign, orders, offsets):
    height, width = left_rows.shape
    band = right_rows.shape[1] * lax.axis_size("tile")
    block = band // lax.axis_size("blk")
    dma = pltpu.SemaphoreType.DMA
    vmem = pl.BlockSpec(memory_space=pltpu.VMEM)
    hbm = pl.BlockSpec(memory_space=pl.ANY)
    return pl.pallas_call(
        kernel,
        out_shape=pltpu.VMEM((block, width), BF16),
        in_specs=[hbm] * 7,
        out_specs=vmem,
        scratch_shapes=[
            *[pltpu.SMEM(assign.shape, jnp.int32)] * 3,
            pltpu.VMEM((1, height), F32), pltpu.VMEM((1, height), F32), pltpu.VMEM(right_rows.shape, BF16),
            pltpu.VMEM((4, height, width), BF16),
            pltpu.VMEM((PLANS, block, 4 * height), BF16),
            pltpu.VMEM((block, 8 * height), BF16),
            pltpu.VMEM((right_rows.shape[1], height), BF16),
            pltpu.VMEM((4, 4, right_rows.shape[1] // 4, height), BF16),
            pltpu.VMEM((block, width), BF16),
            pltpu.VMEM((block, width), BF16),
            pltpu.VMEM((block, width), F32),
            dma((PLANS, STEPS, 2)), dma((PLANS, STEPS, 2)),
            dma((PLANS, STEPS, 2)), dma((PLANS, STEPS, 2)),
            dma((PLANS, STEPS, 2)), dma((PLANS, STEPS, 2)),
            dma((6,)), dma((2,)), dma((3,)), dma((3,)), dma((2, 2)), dma((2, 2)), dma((2, 2)), dma((2, 2)),
            dma((PLANS + 1, 7)), dma((PLANS + 1,)), dma((2,)),
            dma((PLANS + 1, 2)), dma((PLANS + 1, 2)),
            dma((PLANS + 1, 2)), dma((PLANS + 1, 2)),
            dma((PLANS + 1, 4)), dma((PLANS + 1, 4)),
        ],
        compiler_params=pltpu.CompilerParams(collective_id=0, has_side_effects=True, vmem_limit_bytes=60 * 2**20),
    )(
        assign, orders, offsets, row_weight.reshape(1, height), coupling.reshape(1, height), right_rows, left_rows
    )


def solution(mesh):
    return jax.shard_map(
        shards,
        mesh=mesh,
        in_specs=(P("blk", "tile"), P("blk", "tile"), P("blk"), P("blk"), P(), P(), P()),
        out_specs=P("blk", "tile"),
        check_vma=False,
    )
```

```python
import functools

import jax
import jax.numpy as jnp
from jax import lax
from jax.experimental import pallas as pl
from jax.experimental.pallas import tpu as pltpu
from jax.sharding import PartitionSpec as P

MESH = pl.DeviceIdType.MESH
F32 = jnp.float32
BF16 = jnp.bfloat16
HIGH = lax.Precision.HIGHEST
PLANS = 3
OWN = 3
SHIFTED = 3
FORWARD_ROWS = ((112, 144), (144, 112), (128, 128))
STEPS = 4


def flip(bit):
    return 1 - bit


def differ(one, other):
    return (one + other) % 2


def ring_bits(place):
    high = place // 2
    return (place + high) % 2, high


def ring_place(low, high):
    return 2 * high + (low + high) % 2


def blk_bits(index):
    low, high = ring_bits(index % 4)
    return low, high, index // 4


def blk_index(bits):
    return bits[2] * 4 + ring_place(bits[0], bits[1])


def weigh(mine, assign, orders, offsets, row_weight, coupling, right):
    n_rows = right.shape[0]
    n_blocks = assign.shape[0]
    slots = lax.broadcasted_iota(jnp.int32, (1, n_rows), 1)
    members, scaled = [], []
    for block in range(n_blocks):
        start = offsets[block]
        inside = (
            (jnp.full((1, n_rows), assign[block], jnp.int32) == mine)
            & (slots >= start)
            & (slots < start + orders[block])
        ).astype(F32)
        members.append(inside)
        scaled.append(inside / jnp.sqrt(jnp.full((1, n_rows), orders[block], jnp.int32).astype(F32)))
    member = jnp.concatenate(members, axis=0)
    shares = jnp.concatenate(scaled, axis=0)
    right_t = right[...].astype(F32).T
    sums = lax.dot_general(
        right_t * coupling[...], member, (((1,), (1,)), ((), ())), precision=HIGH, preferred_element_type=F32
    )
    spread = lax.dot_general(
        sums, shares, (((1,), (0,)), ((), ())), precision=HIGH, preferred_element_type=F32
    )
    live = jnp.sum(member, axis=0, keepdims=True)
    return (live * row_weight[...] * right_t + coupling[...] * spread).astype(BF16)


def kernel(
    assign_in, orders_in, offsets_in, row_weight_in, coupling_in, right_in, left, out,
    assign, orders, offsets, row_weight, coupling, right,
    slabs, weights, own_weights, piece, quarters, partial, arrived, total,
    own_send, own_recv, fwd_send, fwd_recv, sum_send, sum_recv,
    small_sem, local_sem, part_send, part_recv, z_send, z_recv, zf_send, zf_recv, put_send, put_recv, chain_send,
    x_send, x_recv, xf_send, xf_recv, core_send, core_recv,
):
    height, width = left.shape
    plan_width = width // PLANS
    step_width = plan_width // STEPS
    block = weights.shape[1]
    core_rows = block // 2
    x_rows = core_rows // 4
    blk = lax.axis_index("blk")
    tile = lax.axis_index("tile")
    x, z_hi, core = tile // 4, (tile // 2) % 2, tile % 2
    y, z = blk % 4, z_hi * 2 + blk // 4
    bits = blk_bits(blk)
    x_bits, z_bits = ring_bits(x), ring_bits(z)

    def device(x_to, y_to, z_to, core_to):
        return (z_to % 2) * 4 + y_to, x_to * 4 + (z_to // 2) * 2 + core_to

    def across(dim):
        return blk_index([flip(bit) if at == dim else bit for at, bit in enumerate(bits)]), tile

    def moved(place_bits, *flips):
        return ring_place(*[differ(bit, by) for bit, by in zip(place_bits, flips)])

    x_near = [moved(x_bits, 1, 0), moved(x_bits, 0, 1)]
    x_far = moved(x_bits, 1, 1)
    z_near = [moved(z_bits, 1, 0), moved(z_bits, 0, 1)]
    y_bits = bits[:2]
    x_peers = [device(to, y, z, core) for to in (*x_near, x_far)]
    z_peers = [device(x, y, to, core) for to in z_near]
    y_peers = {by: device(x, moved(y_bits, *by), z, core) for by in ((1, 0), (0, 1), (1, 1))}
    twin = device(x, y, z, 1 - core)

    barrier = pltpu.get_barrier_semaphore()
    peers = [*y_peers.values(), *z_peers, *x_peers, twin]
    for peer in peers:
        pl.semaphore_signal(barrier, inc=1, device_id=peer, device_id_type=MESH)
    local = pltpu.make_async_copy(left, slabs.at[0], local_sem.at[0])
    local.start()
    small = ((assign_in, assign), (orders_in, orders), (offsets_in, offsets),
             (row_weight_in, row_weight), (coupling_in, coupling), (right_in, right))
    fetches = [pltpu.make_async_copy(src, dst, small_sem.at[at]) for at, (src, dst) in enumerate(small)]
    for fetch in fetches:
        fetch.start()
    for fetch in fetches:
        fetch.wait()
    piece[...] = weigh(blk, assign, orders, offsets, row_weight, coupling, right)
    pl.semaphore_wait(barrier, len(peers))

    def remote(src, dst, send, recv, peer):
        return pltpu.make_async_remote_copy(
            src_ref=src, dst_ref=dst, send_sem=send, recv_sem=recv,
            device_id=peer, device_id_type=MESH,
        )

    def columns(plan, step):
        return pl.ds(pl.multiple_of(plan * plan_width + step * step_width, step_width), step_width)

    def own_copy(plan, step, side):
        cols = columns(plan, step)
        return remote(
            left.at[:, cols], slabs.at[1 + side, :, cols],
            own_send.at[plan, step, side], own_recv.at[plan, step, side],
            across((plan + 1 + side) % 3),
        )

    def fwd_copy(plan, step, side):
        cols = columns(plan, step)
        shares = FORWARD_ROWS[plan] if step < SHIFTED else (128, 128)
        rows = pl.ds(side * shares[0], shares[side])
        return remote(
            slabs.at[2 - side, rows, cols], slabs.at[3, rows, cols],
            fwd_send.at[plan, step, side], fwd_recv.at[plan, step, side],
            across((plan + 1 + side) % 3),
        )

    def sum_copy(plan, step, part):
        cols = columns(plan, step)
        rows = pl.ds(part * core_rows, core_rows)
        return remote(
            partial.at[rows, cols], arrived.at[rows, cols],
            sum_send.at[plan, step, part], sum_recv.at[plan, step, part], across(plan),
        )

    def send_own(step, *sent):
        for plan, side in sent:
            own_copy(plan, step, side).start()

    over_y = ((0, 0), (1, 1), (2, 0), (2, 1))
    send_own(0, *over_y, (0, 1))


    def quarter(index):
        return piece.at[pl.ds(pl.multiple_of(index * x_rows, x_rows), x_rows), :]

    def part_copy(index):
        place = (*x_near, x_far)[index]
        return remote(
            quarter(place), quarters.at[z, x], part_send.at[index], part_recv.at[index], x_peers[index]
        )

    kept = pltpu.make_async_copy(quarter(x), quarters.at[z, x], local_sem.at[1])
    for index in range(3):
        part_copy(index).start()
    kept.start()

    plane = bits[2]

    def z_copies(side):
        for at, part in enumerate((pl.ds(2 * flip(plane), 2), pl.ds(2 * plane + side, 1))):
            region = quarters.at[z, part]
            yield remote(region, region, z_send.at[side, at], z_recv.at[side, at], z_peers[side])

    def zf_copies(side):
        for at, place in enumerate((plane, flip(plane))):
            region = quarters.at[z_near[1 - side], 2 * place + 1 - side]
            yield remote(region, region, zf_send.at[side, at], zf_recv.at[side, at], z_peers[side])

    def each(copies, act):
        for side in range(2):
            for copy in copies(side):
                getattr(copy, act)()

    kept.wait()
    for index in range(3):
        part_copy(index).wait_recv()
    each(z_copies, "start")

    def puts(unit):
        if unit == OWN:
            for slot in (0, 1, 2, 4, 5, 6):
                move = (slot % 2, slot // 2 % 2)
                band = [differ(bits[0], move[0]), differ(bits[1], move[1])]
                yield move, differ(plane, slot // 4), band, plane, slot
            return
        for first in range(2):
            for second in range(2):
                if unit < 2:
                    far, slab_plane = first, second
                    band, move = [None, None], [None, None]
                    band[unit], band[1 - unit] = flip(bits[unit]), differ(bits[1 - unit], far)
                    move[unit], move[1 - unit] = 0, far
                    apart = differ(slab_plane, plane)
                    yield tuple(move), slab_plane, band, plane, apart + 2 * far if unit == 1 else far + 2 * apart
                else:
                    band = [differ(bits[0], first), differ(bits[1], second)]
                    yield (first, second), plane, band, flip(plane), first + 2 * second

    def store(unit):
        return own_weights if unit == OWN else weights.at[unit]

    def x_region(unit, x_from, first, count):
        start = pl.multiple_of(core * core_rows + x_from * x_rows + first, count)
        rows = pl.ds(start, count)
        return own_weights.at[rows, pl.ds(0, 7 * height)] if unit == OWN else weights.at[unit, rows, :]

    def put_copies(unit, with_local):
        for index, (move, slab_plane, band, band_plane, slot) in enumerate(puts(unit)):
            band_z_hi = differ(band[0], band[1])
            band_x = 2 * band_plane + band[1]
            rows = pl.ds(pl.multiple_of(core * core_rows + x * x_rows, x_rows), x_rows)
            lanes = pl.ds(pl.multiple_of(slot * height, height), height)
            src = quarters.at[band_z_hi * 2 + slab_plane, band_x]
            dst = store(unit).at[rows, lanes]
            if move != (0, 0):
                yield remote(src, dst, put_send.at[unit, index], put_recv.at[unit], y_peers[move])
            elif with_local:
                yield pltpu.make_async_copy(src, dst, put_recv.at[unit])

    def chain_copy(side):
        count = x_rows // 2
        start = pl.multiple_of(core * core_rows + x * x_rows + side * count, count)
        rows = pl.ds(start, count)
        return remote(
            weights.at[1 - side, rows, pl.ds((2 - side) * height, height)],
            own_weights.at[rows, pl.ds(3 * height, height)],
            chain_send.at[side], put_recv.at[OWN], y_peers[(side, 1 - side)],
        )

    def x_copy(unit, side):
        region = x_region(unit, x, 0, x_rows)
        return remote(region, region, x_send.at[unit, side], x_recv.at[unit, side], x_peers[side])

    def xf_copy(unit, side):
        region = x_region(unit, x_near[1 - side], side * (x_rows // 2), x_rows // 2)
        return remote(region, region, xf_send.at[unit, side], xf_recv.at[unit, side], x_peers[side])

    def core_copy(unit, index):
        region = x_region(unit, (x, *x_near, x_far)[index], 0, x_rows)
        return remote(region, region, core_send.at[unit, index], core_recv.at[unit, index], twin)

    def x_begin(unit):
        region = x_region(unit, x, 0, x_rows)
        pltpu.make_async_copy(region, region, put_recv.at[unit]).wait()
        for side in range(2):
            x_copy(unit, side).start()
        core_copy(unit, 0).start()

    def x_pass(unit):
        for side in range(2):
            x_copy(unit, side).wait_recv()
        for side in range(2):
            xf_copy(unit, side).start()
        for index in (1, 2):
            core_copy(unit, index).start()

    def x_end(unit):
        for side in range(2):
            xf_copy(unit, side).wait_recv()
        core_copy(unit, 3).start()

    def core_end(unit):
        for index in range(4):
            core_copy(unit, index).wait_recv()

    def forward(step):
        for plan in range(PLANS):
            for side in range(2):
                own_copy(plan, step, side).wait_recv()
            for side in range(2):
                fwd_copy(plan, step, side).start()

    send_own(0, (1, 0))
    send_own(1, *over_y)
    each(z_copies, "wait_recv")
    each(zf_copies, "start")
    send_own(1, (0, 1), (1, 0))
    send_own(2, (2, 0), (2, 1))
    each(zf_copies, "wait_recv")
    for unit in range(PLANS):
        for copy in put_copies(unit, True):
            copy.start()
    send_own(2, (0, 0), (1, 1), (0, 1), (1, 0))
    forward(0)
    for unit in range(PLANS):
        x_begin(unit)
    send_own(3, *over_y, (0, 1), (1, 0))
    forward(1)
    for unit in range(PLANS):
        x_pass(unit)
    forward(2)
    for copy in put_copies(OWN, True):
        copy.start()
    for side in range(2):
        chain_copy(side).start()
    for unit in range(PLANS):
        x_end(unit)
    forward(3)
    x_begin(OWN)
    for unit in range(PLANS):
        core_end(unit)
    local.wait()

    def partner_product(plan, cols):
        rows = slabs[:, :, cols].reshape(4 * height, step_width)
        return jnp.dot(weights[plan], rows, preferred_element_type=F32)

    def own_product(plan, cols):
        result = None
        for slot in range(4):
            apart = (slot % 2) * 2 ** ((plan + 1) % 3) + (slot // 2) * 2 ** ((plan + 2) % 3)
            lanes = pl.ds(apart * height, height)
            term = jnp.dot(own_weights[:, lanes], slabs[slot, :, cols], preferred_element_type=F32)
            result = term if result is None else result + term
        return result

    for step in range(STEPS):
        for plan in (2, 0, 1):
            cols = columns(plan, step)
            for side in range(2):
                fwd_copy(plan, step, side).wait_recv()
            partial[:, cols] = partner_product(plan, cols).astype(BF16)
            for part in range(2):
                sum_copy(plan, step, part).start()

    for stage in (x_pass, x_end, core_end):
        stage(OWN)

    @pl.loop(0, STEPS)
    def _(step):
        for plan in range(PLANS):
            cols = columns(plan, step)
            total[:, cols] = own_product(plan, cols)

    for index in range(3):
        part_copy(index).wait_send()
    each(z_copies, "wait_send")
    for side in range(2):
        chain_copy(side).wait_send()
    each(zf_copies, "wait_send")
    for unit in range(PLANS + 1):
        for copy in put_copies(unit, False):
            copy.wait_send()
        for side in range(2):
            x_copy(unit, side).wait_send()
            xf_copy(unit, side).wait_send()
        for index in range(4):
            core_copy(unit, index).wait_send()

    for step in range(STEPS):
        for plan in range(PLANS):
            for side in range(2):
                own_copy(plan, step, side).wait_send()
                fwd_copy(plan, step, side).wait_send()

    @pl.loop(0, STEPS)
    def _(step):
        for part in range(2):
            rows = pl.ds(part * core_rows, core_rows)
            for plan in range(PLANS):
                cols = columns(plan, step)
                sum_copy(plan, step, part).wait()
                out[rows, cols] = (total[rows, cols] + arrived[rows, cols].astype(F32)).astype(BF16)


def shards(left_rows, right_rows, row_weight, coupling, assign, orders, offsets):
    height, width = left_rows.shape
    band = right_rows.shape[1] * lax.axis_size("tile")
    block = band // lax.axis_size("blk")
    dma = pltpu.SemaphoreType.DMA
    vmem = pl.BlockSpec(memory_space=pltpu.VMEM)
    hbm = pl.BlockSpec(memory_space=pl.ANY)
    return pl.pallas_call(
        kernel,
        out_shape=pltpu.VMEM((block, width), BF16),
        in_specs=[hbm] * 7,
        out_specs=vmem,
        scratch_shapes=[
            *[pltpu.SMEM(assign.shape, jnp.int32)] * 3,
            pltpu.VMEM((1, height), F32), pltpu.VMEM((1, height), F32), pltpu.VMEM(right_rows.shape, BF16),
            pltpu.VMEM((4, height, width), BF16),
            pltpu.VMEM((PLANS, block, 4 * height), BF16),
            pltpu.VMEM((block, 8 * height), BF16),
            pltpu.VMEM((right_rows.shape[1], height), BF16),
            pltpu.VMEM((4, 4, right_rows.shape[1] // 4, height), BF16),
            pltpu.VMEM((block, width), BF16),
            pltpu.VMEM((block, width), BF16),
            pltpu.VMEM((block, width), F32),
            dma((PLANS, STEPS, 2)), dma((PLANS, STEPS, 2)),
            dma((PLANS, STEPS, 2)), dma((PLANS, STEPS, 2)),
            dma((PLANS, STEPS, 2)), dma((PLANS, STEPS, 2)),
            dma((6,)), dma((2,)), dma((3,)), dma((3,)), dma((2, 2)), dma((2, 2)), dma((2, 2)), dma((2, 2)),
            dma((PLANS + 1, 7)), dma((PLANS + 1,)), dma((2,)),
            dma((PLANS + 1, 2)), dma((PLANS + 1, 2)),
            dma((PLANS + 1, 2)), dma((PLANS + 1, 2)),
            dma((PLANS + 1, 4)), dma((PLANS + 1, 4)),
        ],
        compiler_params=pltpu.CompilerParams(collective_id=0, has_side_effects=True, vmem_limit_bytes=60 * 2**20),
    )(
        assign, orders, offsets, row_weight.reshape(1, height), coupling.reshape(1, height), right_rows, left_rows
    )


def solution(mesh):
    return jax.shard_map(
        shards,
        mesh=mesh,
        in_specs=(P("blk", "tile"), P("blk", "tile"), P("blk"), P("blk"), P(), P(), P()),
        out_specs=P("blk", "tile"),
        check_vma=False,
    )
```
